32 devices in a mesh: blk: 32 (over z, y, x, core).
Axes of the slice: x: 2, y: 2, z: 4, core: 2. Of those that a mesh axis runs over, the one named last changes fastest.
Arguments:
- old_phase: float32 [512, 32768], P('blk'), may hold values from -1 to 1
- old_solute: float32 [512, 32768], P('blk'), may hold values from -0.45 to 0.45
- old_mobility: float32 [512, 32768], P('blk'), may hold values from 0.25 to 1
- new_global_slot: int32 [512], P('blk'), may hold values from -1 to 255, as said below
- neighbors: int32 [256, 6], P('blk'), may hold values from -1 to 255, as said below
Outputs:
- phase: float32 [256, 32768], P('blk')
- solute: float32 [256, 32768], P('blk')
The draws below stay inside these ranges and needn't reach their ends.
Inputs may be any that keep to these rules, and one draw needn't show every extreme that they name: Each device's old slots hold its blocks first and -1 after them; the blocks taken in device order and slot order get the consecutive numbers 0 to 255. The block in an old slot of device p goes to device new_global_slot // 8, at most 2 devices away; in every draw some block moves exactly 2 devices down and some exactly 2 up, some device holds 16 blocks and some none. `neighbors`: the relation is symmetric: if b is the +x (+y, +z) neighbour of a, then a is the -x (-y, -z) neighbour of b. The x neighbours of a block of device p lie on devices p - 1 and p + 1 (every block has both except on the first and last device, where that side is -1); y and z neighbours lie on the block's own device, with -1 at the ends along y and none along z (a block may be its own z neighbour). The layers of blocks line up: if b is the -x (+x) neighbour of a, then the y and z neighbours of b are the -x (+x) neighbours of the y and z neighbours of a, and -1 where those are -1.
All inputs are finite; a program needn't handle non-finite values.
Results may differ from the reference program's by a relative error of at most 0.00014.
Values sent between devices are 32-bit elements; how exact they have to be, the bound alone decides.
A program may use at most 128 MiB of HBM per device.

```python
import math
import jax
import jax.numpy as jnp
from jax import lax

BLOCK_EDGE_CELLS = 32
BLOCK_CELLS = 32768
FACE_CELLS = 1024
CAP = 8
SPREAD = 2
STEPS = 3
ACTIVE_BLOCKS = 256
NOLD = 512
N_BLK = 32


def draw_old_phase(key, part):
    cell_ids = jnp.arange(BLOCK_CELLS)
    xs = (cell_ids // FACE_CELLS).astype(jnp.float32)
    ys = (cell_ids // BLOCK_EDGE_CELLS % BLOCK_EDGE_CELLS).astype(jnp.float32)
    zs = (cell_ids % BLOCK_EDGE_CELLS).astype(jnp.float32)
    middle = (BLOCK_EDGE_CELLS - 1) / 2.0
    inverse_width = 1.0 / (math.sqrt(2.0) * BLOCK_EDGE_CELLS / 8.0)
    rough = jax.random.uniform(jax.random.fold_in(key, 31), (NOLD, BLOCK_CELLS), jnp.float32, -1.0, 1.0)
    azimuth = jax.random.uniform(jax.random.fold_in(key, 34), (NOLD, 1), jnp.float32, 0.0, 2.0 * math.pi)
    polar = jax.random.uniform(jax.random.fold_in(key, 35), (NOLD, 1), jnp.float32, 0.0, math.pi)
    shift_along = jax.random.uniform(jax.random.fold_in(key, 36), (NOLD, 1), jnp.float32, -BLOCK_EDGE_CELLS / 4.0, BLOCK_EDGE_CELLS / 4.0)
    normal_x = jnp.cos(azimuth) * jnp.sin(polar)
    normal_y = jnp.sin(azimuth) * jnp.sin(polar)
    normal_z = jnp.cos(polar)
    distance = normal_x * (xs[None, :] - middle) + normal_y * (ys[None, :] - middle) + normal_z * (zs[None, :] - middle) - shift_along
    phase = 0.92 * jnp.tanh(distance * inverse_width) + 0.08 * rough
    return phase.astype(jnp.float32)


def draw_new_global_slot(key, part):
    groups = N_BLK // (2 * SPREAD)
    depth = jax.random.randint(jax.random.fold_in(key, 1), (groups, SPREAD), 0, CAP + 1)
    flips = jax.random.randint(jax.random.fold_in(key, 2), (groups,), 0, 2)
    first = jax.random.randint(jax.random.fold_in(key, 3), (), 0, groups - 1)
    second = groups - 1
    group_ids = jnp.arange(groups)
    forced = (group_ids == first) | (group_ids == second)
    depth = jnp.where(forced[:, None], CAP, depth)
    flips = jnp.where(group_ids == first, 0, jnp.where(group_ids == second, 1, flips))
    signs = 1 - 2 * flips
    lower = CAP - signs[:, None] * depth
    upper = CAP + signs[:, None] * depth[:, ::-1]
    counts = jnp.concatenate([lower, upper], axis=1).reshape(N_BLK)
    starts = jnp.cumsum(counts) - counts
    slot_ids = jnp.arange(2 * CAP)
    result = jnp.where(slot_ids[None, :] < counts[:, None], starts[:, None] + slot_ids[None, :], -1)
    return result.reshape(NOLD).astype(jnp.int32)


def device_perms(key):
    return jax.vmap(lambda sub: jax.random.permutation(sub, CAP))(jax.random.split(key, N_BLK))


def draw_neighbors(key, part):
    columns = max(1, min(2, CAP // 2))
    rows_y = CAP // columns
    dev_ids = jnp.arange(N_BLK)[:, None]
    position = device_perms(jax.random.fold_in(key, 11))
    inverse = jnp.argsort(position, axis=1)
    prev_inverse = jnp.concatenate([inverse[:1], inverse[:-1]], axis=0)
    next_inverse = jnp.concatenate([inverse[1:], inverse[-1:]], axis=0)
    row_pos = position // columns
    col_pos = position % columns
    minus_x = jnp.where(dev_ids > 0, (dev_ids - 1) * CAP + jnp.take_along_axis(prev_inverse, position, axis=1), -1)
    plus_x = jnp.where(dev_ids < N_BLK - 1, (dev_ids + 1) * CAP + jnp.take_along_axis(next_inverse, position, axis=1), -1)
    here = dev_ids * CAP
    minus_y = jnp.where(row_pos > 0, here + jnp.take_along_axis(inverse, jnp.clip(position - columns, 0, CAP - 1), axis=1), -1)
    plus_y = jnp.where(row_pos < rows_y - 1, here + jnp.take_along_axis(inverse, jnp.clip(position + columns, 0, CAP - 1), axis=1), -1)
    minus_z = here + jnp.take_along_axis(inverse, row_pos * columns + (col_pos + columns - 1) % columns, axis=1)
    plus_z = here + jnp.take_along_axis(inverse, row_pos * columns + (col_pos + 1) % columns, axis=1)
    lookup_table = jnp.stack([minus_x, plus_x, minus_y, plus_y, minus_z, plus_z], axis=-1)
    return lookup_table.reshape(ACTIVE_BLOCKS, 6).astype(jnp.int32)


def shard_levels(own_key, shape, pieces, least, largest):
    factor_of, own = 1.0, jax.random.fold_in(own_key, 6)
    for dim, blocks in pieces:
        heights = jnp.exp(jax.random.uniform(jax.random.fold_in(own, dim), (blocks,), jnp.float32, least / len(pieces), largest / len(pieces)))
        factor_of = factor_of * jnp.repeat(heights, shape[dim] // blocks).reshape([-1 if axis == dim else 1 for axis in range(len(shape))])
    return factor_of


def noise(own_key, extent, width, limit, pieces=(), held_as=jnp.bfloat16):
    factor_of = shard_levels(own_key, extent, pieces, -0.22, 0.18) if pieces else 1.0
    array = jax.random.normal(own_key, extent, jnp.float32) * width * factor_of
    return jnp.minimum(jnp.maximum(array, -limit), limit).astype(held_as)


def setup_inputs(seed: int = 0) -> dict:
    key_of = jax.random.split(jax.random.key(seed), 6)
    return {
        "old_phase": draw_old_phase(jax.random.fold_in(key_of[5], 71), 0),
        "old_solute": noise(key_of[1], (NOLD, BLOCK_CELLS), 0.15, 0.45, ((0, 32),), jnp.float32),
        "old_mobility": jnp.clip(jnp.exp(math.log(1.0) - 1.3862944 * jax.random.uniform(key_of[2], (NOLD, BLOCK_CELLS), jnp.float32) ** shard_levels(key_of[2], (NOLD, BLOCK_CELLS), ((0, 32),), -0.2, 0.2)), 0.25, 1.0),
        "new_global_slot": draw_new_global_slot(jax.random.fold_in(key_of[5], 71), 0),
        "neighbors": draw_neighbors(jax.random.fold_in(key_of[5], 71), 0),
    }


time_step = 0.15
coupling = 1.5


def block_faces(field_arrays):
    edge = field_arrays.shape[2]
    low_x = field_arrays[:, :, 0, :]
    high_x = field_arrays[:, :, edge - 1, :]
    low_y = field_arrays[:, :, :, :edge]
    high_y = field_arrays[:, :, :, -edge:]
    low_z = field_arrays[:, :, :, 0::edge]
    high_z = field_arrays[:, :, :, edge - 1::edge]
    return low_x, high_x, low_y, high_y, low_z, high_z


def pick_face(other, own, index):
    valid = index >= 0
    taken = jnp.take(other, jnp.maximum(index, 0), axis=0)
    return jnp.where(valid.reshape((-1,) + (1,) * (own.ndim - 1)), taken, own)


def laplacian(field_arrays, ghosts):
    minus_x, plus_x, minus_y, plus_y, minus_z, plus_z = ghosts
    edge = field_arrays.shape[2]
    flat_ids = jnp.arange(field_arrays.shape[3], dtype=jnp.int32)
    y_ids = flat_ids // edge
    z_ids = flat_ids % edge
    prev_x = jnp.concatenate([minus_x[:, :, None, :], field_arrays[:, :, :-1, :]], axis=2)
    next_x = jnp.concatenate([field_arrays[:, :, 1:, :], plus_x[:, :, None, :]], axis=2)
    zero_row = jnp.zeros(field_arrays.shape[:3] + (edge,), jnp.float32)
    zero_one = jnp.zeros(field_arrays.shape[:3] + (1,), jnp.float32)
    prev_y = jnp.where(y_ids == 0, jnp.tile(minus_y, (1, 1, 1, edge)),
                       jnp.concatenate([zero_row, field_arrays[..., :-edge]], axis=-1))
    next_y = jnp.where(y_ids == edge - 1, jnp.tile(plus_y, (1, 1, 1, edge)),
                       jnp.concatenate([field_arrays[..., edge:], zero_row], axis=-1))
    prev_z = jnp.where(z_ids == 0, jnp.repeat(minus_z, edge, axis=-1),
                       jnp.concatenate([zero_one, field_arrays[..., :-1]], axis=-1))
    next_z = jnp.where(z_ids == edge - 1, jnp.repeat(plus_z, edge, axis=-1),
                       jnp.concatenate([field_arrays[..., 1:], zero_one], axis=-1))
    return (prev_x + next_x) + (prev_y + next_y) + (prev_z + next_z) - 6.0 * field_arrays


def advance(field_arrays, mobility, ghosts):
    lapl = laplacian(field_arrays, ghosts)
    phi = field_arrays[:, 0]
    conc = field_arrays[:, 1]
    wetting = 1.0 - phi * phi
    drive = lapl[:, 0] + phi - phi * phi * phi - coupling * conc * wetting * wetting
    new_phi = phi + time_step * mobility * drive
    new_conc = conc + time_step * lapl[:, 1] + 0.5 * (new_phi - phi)
    return jnp.stack([new_phi, new_conc], axis=1)


def reference(old_phase, old_solute, old_mobility, new_global_slot, neighbors):
    stacked_fields = jnp.stack([old_phase, old_solute, old_mobility], axis=1)
    target_slot = jnp.where(new_global_slot >= 0, new_global_slot, ACTIVE_BLOCKS).astype(jnp.int32)
    placed_blocks = jnp.zeros((ACTIVE_BLOCKS, 3, BLOCK_CELLS), jnp.float32).at[target_slot].set(stacked_fields, mode="drop")
    placed_blocks = placed_blocks.reshape(ACTIVE_BLOCKS, 3, BLOCK_EDGE_CELLS, FACE_CELLS)
    field_arrays = placed_blocks[:, :2]
    mobility = placed_blocks[:, 2]
    for step in range(STEPS):
        low_x, high_x, low_y, high_y, low_z, high_z = block_faces(field_arrays)
        ghosts = (pick_face(high_x, low_x, neighbors[:, 0]), pick_face(low_x, high_x, neighbors[:, 1]),
                  pick_face(high_y, low_y, neighbors[:, 2]), pick_face(low_y, high_y, neighbors[:, 3]),
                  pick_face(high_z, low_z, neighbors[:, 4]), pick_face(low_z, high_z, neighbors[:, 5]))
        grouped = jax.tree.map(lambda a: a.reshape((N_BLK, CAP) + a.shape[1:]), (field_arrays, mobility, ghosts))
        result = lax.map(lambda t: advance(t[0], t[1], t[2]), grouped)
        field_arrays = result.reshape(field_arrays.shape)
    return field_arrays[:, 0].reshape(ACTIVE_BLOCKS, BLOCK_CELLS), field_arrays[:, 1].reshape(ACTIVE_BLOCKS, BLOCK_CELLS)
```

```python
import functools

import jax
import jax.numpy as jnp
from jax import lax
from jax.experimental import pallas as pl
from jax.experimental.pallas import tpu as pltpu
from jax.sharding import PartitionSpec as P

EDGE = 32
STEPS = 3
FIELDS = 3
SUB = 8
LANES = 128
AHEAD = 2
LAG = 4
SETTLE = 3

time_step = 0.15
coupling = 1.5


def kernel(n, cap, nold, ngs, nbs, op, oc, om, phi_out, conc_out, old,
           side_s, side_r, pair_s, pair_r, far_s, far_r, near_s, near_r,
           fld0, fld1, fld2, mob, ghost0, ghost1, ghost2, lsem, ssem, rsem, hs, hr):
    flds = (fld0, fld1, fld2)
    ghosts = (ghost0, ghost1, ghost2)
    rows = EDGE * SUB
    span = nold * rows
    loads = [
        pltpu.make_async_copy(src, old.at[pl.ds(f * span, span)], lsem.at[f])
        for f, src in enumerate((op, oc, om))
    ]
    for copy in loads:
        copy.start()

    me = lax.axis_index("blk")
    core = me % 2
    odd = (me // 2) % 2
    sib = me + 1 - 2 * core
    near = me + 2 - 4 * odd
    far_final = me - 2 + 4 * odd
    far = me - 4 + 8 * odd
    far_source = me + 4 - 8 * odd
    side_final = me - 1 + 2 * core
    up, down = me + 1, me - 1
    has_up, has_down = up < n, down >= 0
    sends_far = (far_final >= 0) & (far_final < n)
    gets_far = (far_source >= 0) & (far_source < n)

    barrier = pltpu.get_barrier_semaphore()
    expected = jnp.int32(0)
    for other, there in ((up, has_up), (down, has_down), (near, None), (far, sends_far), (far_source, gets_far)):
        def greet(other=other):
            pl.semaphore_signal(barrier, inc=1, device_id=(other,), device_id_type=pl.DeviceIdType.MESH)
        if there is None:
            greet()
            expected = expected + 1
        else:
            pl.when(there)(greet)
            expected = expected + there.astype(jnp.int32)

    start = ngs[0]
    count = jnp.int32(0)
    for s in range(nold):
        count = count + (ngs[s] >= 0).astype(jnp.int32)

    def plane(k):
        half = lax.div(k, 2)
        return jnp.where(lax.rem(k, 2) == 0, half, EDGE - 1 - half)

    def held(k, final, put):
        x = plane(k)
        for j in range(cap):
            idx = final * cap + j - start
            mine = (idx >= 0) & (idx < count)
            idx = jnp.clip(idx, 0, nold - 1)
            row = lax.div(idx, SUB) * (rows * SUB) + lax.rem(idx, SUB) + x * (SUB * SUB)
            for f in range(FIELDS):
                got = old[pl.ds(f * span + row, SUB, stride=SUB), :]
                put(f, j, x, jnp.where(mine, got, 0.0))

    def link(stream, src, dst, k, target):
        return pltpu.make_async_remote_copy(
            src_ref=src.at[k], dst_ref=dst.at[k],
            send_sem=ssem.at[stream, k], recv_sem=rsem.at[stream, k],
            device_id=(target,), device_id_type=pl.DeviceIdType.MESH)

    def side_link(k):
        return link(0, side_s, side_r, k, sib)

    def pair_link(k):
        return link(1, pair_s, pair_r, k, sib)

    def far_link(k):
        return link(2, far_s, far_r, k, far)

    def near_link(k):
        return link(3, near_s, near_r, k, near)

    side_goes_far = (core + odd) % 2 == 1

    def fill(buffer, k, final):
        def put(f, j, x, value):
            buffer[k, f, j] = value
        held(k, final, put)

    def send_side(k):
        fill(side_s, k, side_final)
        side_link(k).start()

    def send_pair(k):
        fill(pair_s, k, sib)
        pair_link(k).start()

    def add_side(k, total):
        side_link(k).wait_recv()
        total[k] += side_r[k]

    def send_far(k):
        fill(far_s, k, far_final)
        pl.when(side_goes_far)(lambda: add_side(k, far_s))
        pl.when(sends_far)(lambda: far_link(k).start())

    def send_near(k):
        fill(near_s, k, near)
        pl.when(jnp.logical_not(side_goes_far))(lambda: add_side(k, near_s))

        @pl.when(gets_far)
        def add_far():
            far_link(k).wait_recv()
            near_s[k] += far_r[k]

        near_link(k).start()

    def loop(lo, hi, *bodies):
        def body(i, carry):
            for each in bodies:
                each(i)
            return carry
        lax.fori_loop(lo, hi, body, 0)

    def pipeline(stages, hooks):
        cuts = set(hooks)
        for _, offset, size in stages:
            cuts |= {offset, offset + size}
        cuts = sorted(cuts)
        for lo, hi in zip(cuts, cuts[1:] + cuts[-1:]):
            for act in hooks.get(lo, ()):
                act()
            active = [(body, offset) for body, offset, size in stages if offset <= lo and hi <= offset + size]
            if lo < hi and active:
                loop(lo, hi, *[lambda i, body=body, offset=offset: body(i - offset) for body, offset in active])

    def settle(k):
        pair_link(k).wait_recv()
        near_link(k).wait_recv()

        def put(f, j, x, value):
            value = value + (pair_r[k, f, j] + near_r[k, f, j])
            if f < 2:
                fld0[f, j, x] = value
            else:
                mob[j, x] = value
        held(k, me, put)

    def ghost_link(t, side):
        return pltpu.make_async_remote_copy(
            src_ref=flds[t].at[:, :, 0 if side else EDGE - 1], dst_ref=ghosts[t].at[side],
            send_sem=hs.at[t, side], recv_sem=hr.at[t, side],
            device_id=(down if side else up,), device_id_type=pl.DeviceIdType.MESH)

    def start_ghosts(t):
        pl.when(has_up)(lambda: ghost_link(t, 0).start())
        pl.when(has_down)(lambda: ghost_link(t, 1).start())

    def await_ghosts(t):
        pl.when(has_down)(lambda: ghost_link(t, 0).wait_recv())
        pl.when(has_up)(lambda: ghost_link(t, 1).wait_recv())

    def await_sent(t):
        pl.when(has_up)(lambda: ghost_link(t, 0).wait_send())
        pl.when(has_down)(lambda: ghost_link(t, 1).wait_send())

    lane = lax.broadcasted_iota(jnp.int32, (SUB, LANES), 1)
    row = lax.broadcasted_iota(jnp.int32, (SUB, LANES), 0)
    z = lane % EDGE
    z_low, z_high = z == 0, z == EDGE - 1
    y_first, y_last = lane < EDGE, lane >= LANES - EDGE
    y_start, y_end = y_first & (row == 0), y_last & (row == SUB - 1)

    def local(column, b):
        index = nbs[b, column]
        return lax.rem(jnp.maximum(index, 0), cap), index >= 0

    def advance(t, b, x, beside):
        fld = flds[t]
        at_y0, has_y0 = local(2, b)
        at_y1, has_y1 = local(3, b)
        at_z0, _ = local(4, b)
        at_z1, _ = local(5, b)
        wall_y0 = y_start & jnp.logical_not(has_y0)
        wall_y1 = y_end & jnp.logical_not(has_y1)

        def laplacian(f, here):
            prev_x, next_x = beside(f)
            y0, y1 = fld[f, at_y0, x], fld[f, at_y1, x]
            z0, z1 = fld[f, at_z0, x], fld[f, at_z1, x]
            back = pltpu.roll(jnp.where(y_end, y0, here), EDGE, 1)
            prev_y = jnp.where(y_first, pltpu.roll(back, 1, 0), back)
            prev_y = jnp.where(wall_y0, here, prev_y)
            fore = pltpu.roll(jnp.where(y_start, y1, here), LANES - EDGE, 1)
            next_y = jnp.where(y_last, pltpu.roll(fore, SUB - 1, 0), fore)
            next_y = jnp.where(wall_y1, here, next_y)
            prev_z = jnp.where(z_low, pltpu.roll(z0, LANES - (EDGE - 1), 1), pltpu.roll(here, 1, 1))
            next_z = jnp.where(z_high, pltpu.roll(z1, EDGE - 1, 1), pltpu.roll(here, LANES - 1, 1))
            return (prev_x + next_x) + (prev_y + next_y) + (prev_z + next_z) - 6.0 * here

        phi, conc = fld[0, b, x], fld[1, b, x]
        wetting = 1.0 - phi * phi
        drive = laplacian(0, phi) + phi - phi * phi * phi - coupling * conc * wetting * wetting
        new_phi = phi + time_step * mob[b, x] * drive
        new_conc = conc + time_step * laplacian(1, conc) + 0.5 * (new_phi - phi)
        return new_phi, new_conc

    def keep(t, b, x, new_phi, new_conc):
        if t == STEPS - 1:
            at = (b // SUB) * (rows * SUB) + b % SUB + x * (SUB * SUB)
            phi_out[pl.ds(at, SUB, stride=SUB), :] = new_phi
            conc_out[pl.ds(at, SUB, stride=SUB), :] = new_conc
        else:
            flds[t + 1][0, b, x] = new_phi
            flds[t + 1][1, b, x] = new_conc

    def middle(t, k):
        x = plane(k)
        fld = flds[t]
        results = [advance(t, b, x, lambda f, b=b: (fld[f, b, x - 1], fld[f, b, x + 1])) for b in range(cap)]
        for b, result in enumerate(results):
            keep(t, b, x, *result)

    def ends(t):
        fld, ghost, last = flds[t], ghosts[t], EDGE - 1
        await_ghosts(t)
        results = []
        for b in range(cap):
            at_x0, has_x0 = local(0, b)
            at_x1, has_x1 = local(1, b)
            results.append((b, 0, advance(t, b, 0, lambda f: (
                jnp.where(has_x0, ghost[0, f, at_x0], fld[f, b, 0]), fld[f, b, 1]))))
            results.append((b, last, advance(t, b, last, lambda f: (
                fld[f, b, last - 1], jnp.where(has_x1, ghost[1, f, at_x1], fld[f, b, last])))))
        for b, x, result in results:
            keep(t, b, x, *result)
        if t + 1 < STEPS:
            start_ghosts(t + 1)

    for copy in loads:
        copy.wait()
    pl.semaphore_wait(barrier, expected)
    near_at = AHEAD + LAG
    settle_at = near_at + SETTLE
    stages = [
        (send_side, 0, EDGE),
        (send_far, AHEAD, EDGE),
        (send_near, near_at, EDGE),
        (send_pair, near_at, EDGE),
        (settle, settle_at, EDGE),
    ]
    hooks = {settle_at + 2: (lambda: start_ghosts(0),)}
    for t in range(STEPS):
        begin = settle_at + 2 * (t + 1) + 2
        stages.append((lambda i, t=t: middle(t, i + 2), begin, EDGE - 2))
        when = begin + 2 if t + 1 < STEPS else begin + 4
        hooks[when] = hooks.get(when, ()) + (functools.partial(ends, t),)
    pipeline(stages, hooks)

    def sent(k):
        side_link(k).wait_send()
        pair_link(k).wait_send()
        pl.when(sends_far)(lambda: far_link(k).wait_send())
        near_link(k).wait_send()

    loop(0, EDGE, sent)
    for t in range(STEPS):
        await_sent(t)


def on_device(n, old_phase, old_solute, old_mobility, new_global_slot, neighbors):
    cap = neighbors.shape[0]
    nold, cells = old_phase.shape
    rows = cells // LANES

    def tiled(field):
        split = field.reshape(nold // SUB, SUB, rows, LANES)
        return split.transpose(0, 2, 1, 3).reshape(nold * rows, LANES)

    def flat(field):
        split = field.reshape(cap // SUB, rows, SUB, LANES)
        return split.transpose(0, 2, 1, 3).reshape(cap, cells)

    buffer = pltpu.VMEM((EDGE, FIELDS, cap, SUB, LANES), jnp.float32)
    out = jax.ShapeDtypeStruct((cap * rows, LANES), jnp.float32)
    phase, solute = pl.pallas_call(
        functools.partial(kernel, n, cap, nold),
        out_shape=(out, out),
        in_specs=[pl.BlockSpec(memory_space=pltpu.SMEM)] * 2 + [pl.BlockSpec(memory_space=pl.ANY)] * 3,
        out_specs=[pl.BlockSpec(memory_space=pltpu.VMEM)] * 2,
        scratch_shapes=[pltpu.VMEM((FIELDS * nold * rows, LANES), jnp.float32)] + [buffer] * 8 + [
            pltpu.VMEM((2, cap, EDGE, SUB, LANES), jnp.float32)] * STEPS + [
            pltpu.VMEM((cap, EDGE, SUB, LANES), jnp.float32),
        ] + [pltpu.VMEM((2, 2, cap, SUB, LANES), jnp.float32)] * STEPS + [
            pltpu.SemaphoreType.DMA((FIELDS,)),
            pltpu.SemaphoreType.DMA((4, EDGE)),
            pltpu.SemaphoreType.DMA((4, EDGE)),
            pltpu.SemaphoreType.DMA((STEPS, 2)),
            pltpu.SemaphoreType.DMA((STEPS, 2)),
        ],
        compiler_params=pltpu.CompilerParams(
            collective_id=0, has_side_effects=True, vmem_limit_bytes=56 * 1024 * 1024),
    )(new_global_slot, neighbors, tiled(old_phase), tiled(old_solute), tiled(old_mobility))
    return flat(phase), flat(solute)


def solution(mesh):
    placed = (P("blk", None), P("blk", None), P("blk", None), P("blk"), P("blk", None))
    return jax.shard_map(
        functools.partial(on_device, mesh.shape["blk"]),
        mesh=mesh,
        in_specs=placed,
        out_specs=(P("blk", None), P("blk", None)),
        check_vma=False,
    )
```

```python
import functools

import jax
import jax.numpy as jnp
from jax import lax
from jax.experimental import pallas as pl
from jax.experimental.pallas import tpu as pltpu
from jax.sharding import PartitionSpec as P

EDGE = 32
STEPS = 3
FIELDS = 3
SUB = 8
LANES = 128
AHEAD = 2
LAG = 4
SETTLE = 3
SLACK = 6
EARLY = 8

time_step = 0.15
coupling = 1.5


def plane(k):
    half = k // 2 if isinstance(k, int) else lax.div(k, 2)
    if isinstance(k, int):
        return EDGE - 1 - half if k % 2 else half
    return jnp.where(lax.rem(k, 2) == 0, half, EDGE - 1 - half)


def lag(t):
    return 2 * (t + 1)


def stepper(cap, nbs, flds, mob, phi_out, conc_out, first):
    lane = lax.broadcasted_iota(jnp.int32, (SUB, LANES), 1)
    row = lax.broadcasted_iota(jnp.int32, (SUB, LANES), 0)
    z = lane % EDGE
    z_low, z_high = z == 0, z == EDGE - 1
    y_first, y_last = lane < EDGE, lane >= LANES - EDGE
    y_start, y_end = y_first & (row == 0), y_last & (row == SUB - 1)

    def local(column, b):
        index = nbs[b, column]
        return lax.rem(jnp.maximum(index, 0), cap), index >= 0

    def advance(t, b, x, beside):
        fld = flds[t]
        at_y0, has_y0 = local(2, b)
        at_y1, has_y1 = local(3, b)
        at_z0, _ = local(4, b)
        at_z1, _ = local(5, b)
        wall_y0 = y_start & jnp.logical_not(has_y0)
        wall_y1 = y_end & jnp.logical_not(has_y1)

        def laplacian(f, here):
            prev_x, next_x = beside(f)
            y0, y1 = fld[f, at_y0, x], fld[f, at_y1, x]
            z0, z1 = fld[f, at_z0, x], fld[f, at_z1, x]
            back = pltpu.roll(jnp.where(y_end, y0, here), EDGE, 1)
            prev_y = jnp.where(y_first, pltpu.roll(back, 1, 0), back)
            prev_y = jnp.where(wall_y0, here, prev_y)
            fore = pltpu.roll(jnp.where(y_start, y1, here), LANES - EDGE, 1)
            next_y = jnp.where(y_last, pltpu.roll(fore, SUB - 1, 0), fore)
            next_y = jnp.where(wall_y1, here, next_y)
            prev_z = jnp.where(z_low, pltpu.roll(z0, LANES - (EDGE - 1), 1), pltpu.roll(here, 1, 1))
            next_z = jnp.where(z_high, pltpu.roll(z1, EDGE - 1, 1), pltpu.roll(here, LANES - 1, 1))
            return (prev_x + next_x) + (prev_y + next_y) + (prev_z + next_z) - 6.0 * here

        phi, conc = fld[0, b, x], fld[1, b, x]
        wetting = 1.0 - phi * phi
        drive = laplacian(0, phi) + phi - phi * phi * phi - coupling * conc * wetting * wetting
        new_phi = phi + time_step * mob[b, x] * drive
        new_conc = conc + time_step * laplacian(1, conc) + 0.5 * (new_phi - phi)
        return new_phi, new_conc

    def keep(t, b, x, new_phi, new_conc):
        if t == STEPS - 1:
            at = b % SUB + (x - first) * (SUB * SUB) + (b // SUB) * (phi_out.shape[0] // (cap // SUB))
            phi_out[pl.ds(at, SUB, stride=SUB), :] = new_phi
            conc_out[pl.ds(at, SUB, stride=SUB), :] = new_conc
        else:
            flds[t + 1][0, b, x] = new_phi
            flds[t + 1][1, b, x] = new_conc

    def middle(t, k):
        x = plane(k)
        fld = flds[t]
        results = [advance(t, b, x, lambda f, b=b: (fld[f, b, x - 1], fld[f, b, x + 1])) for b in range(cap)]
        for b, result in enumerate(results):
            keep(t, b, x, *result)

    return local, advance, keep, middle


def kernel(n, cap, nold, ngs, nbs, op, oc, om, phi_out, conc_out, fld0, fld1, fld2, mob, early, late,
           side_s, side_r, pair_s, pair_r, far_s, far_r, near_s, near_r,
           ghost0, ghost1, ghost2, esem, lsem, ssem, rsem, hs, hr):
    flds = (fld0, fld1, fld2)
    ghosts = (ghost0, ghost1, ghost2)
    sheet = SUB * SUB
    tiles = nold // SUB
    edge, inside = EARLY // 2, EDGE - EARLY
    early_loads, late_loads = [], []
    for f, src in enumerate((op, oc, om)):
        for q in range(tiles):
            for side in range(2):
                at = q * EDGE + side * (EDGE - edge)
                early_loads.append(pltpu.make_async_copy(
                    src.at[pl.ds(at * sheet, edge * sheet)],
                    early.at[pl.ds(((f * tiles + q) * EARLY + side * edge) * sheet, edge * sheet)], esem.at[f, q, side]))
            late_loads.append(pltpu.make_async_copy(
                src.at[pl.ds((q * EDGE + edge) * sheet, inside * sheet)],
                late.at[pl.ds((f * tiles + q) * inside * sheet, inside * sheet)], lsem.at[f, q]))
    for copy in early_loads + late_loads:
        copy.start()

    me = lax.axis_index("blk")
    core = me % 2
    odd = (me // 2) % 2
    sib = me + 1 - 2 * core
    near = me + 2 - 4 * odd
    far_final = me - 2 + 4 * odd
    far = me - 4 + 8 * odd
    far_source = me + 4 - 8 * odd
    side_final = me - 1 + 2 * core
    up, down = me + 1, me - 1
    has_up, has_down = up < n, down >= 0
    sends_far = (far_final >= 0) & (far_final < n)
    gets_far = (far_source >= 0) & (far_source < n)

    barrier = pltpu.get_barrier_semaphore()
    expected = jnp.int32(0)
    for other, there in ((up, has_up), (down, has_down), (near, None), (far, sends_far), (far_source, gets_far)):
        def greet(other=other):
            pl.semaphore_signal(barrier, inc=1, device_id=(other,), device_id_type=pl.DeviceIdType.MESH)
        if there is None:
            greet()
            expected = expected + 1
        else:
            pl.when(there)(greet)
            expected = expected + there.astype(jnp.int32)

    start = ngs[0]
    count = jnp.int32(0)
    for s in range(nold):
        count = count + (ngs[s] >= 0).astype(jnp.int32)

    def held(is_early, k, final, put):
        x = plane(k)
        if is_early:
            source, held_planes, at_plane = early, EARLY, jnp.where(x < edge, x, x - inside)
        else:
            source, held_planes, at_plane = late, inside, x - edge
        for j in range(cap):
            idx = final * cap + j - start
            mine = (idx >= 0) & (idx < count)
            idx = jnp.clip(idx, 0, nold - 1)
            row = lax.div(idx, SUB) * (held_planes * sheet) + lax.rem(idx, SUB) + at_plane * sheet
            for f in range(FIELDS):
                got = source[pl.ds(f * (tiles * held_planes * sheet) + row, SUB, stride=SUB), :]
                put(f, j, x, jnp.where(mine, got, 0.0))

    def link(stream, src, dst, k, target):
        return pltpu.make_async_remote_copy(
            src_ref=src.at[k], dst_ref=dst.at[k],
            send_sem=ssem.at[stream, k], recv_sem=rsem.at[stream, k],
            device_id=(target,), device_id_type=pl.DeviceIdType.MESH)

    def side_link(k):
        return link(0, side_s, side_r, k, sib)

    def pair_link(k):
        return link(1, pair_s, pair_r, k, sib)

    def far_link(k):
        return link(2, far_s, far_r, k, far)

    def near_link(k):
        return link(3, near_s, near_r, k, near)

    side_goes_far = (core + odd) % 2 == 1

    def fill(is_early, buffer, k, final):
        def put(f, j, x, value):
            buffer[k, f, j] = value
        held(is_early, k, final, put)

    def send_side(is_early, k):
        fill(is_early, side_s, k, side_final)
        side_link(k).start()

    def send_pair(is_early, k):
        fill(is_early, pair_s, k, sib)
        pair_link(k).start()

    def add_side(k, total):
        side_link(k).wait_recv()
        total[k] += side_r[k]

    def send_far(is_early, k):
        fill(is_early, far_s, k, far_final)
        pl.when(side_goes_far)(lambda: add_side(k, far_s))
        pl.when(sends_far)(lambda: far_link(k).start())

    def send_near(is_early, k):
        fill(is_early, near_s, k, near)
        pl.when(jnp.logical_not(side_goes_far))(lambda: add_side(k, near_s))

        @pl.when(gets_far)
        def add_far():
            far_link(k).wait_recv()
            near_s[k] += far_r[k]

        near_link(k).start()

    def loop(lo, hi, *bodies):
        def body(i, carry):
            for each in bodies:
                each(i)
            return carry
        lax.fori_loop(lo, hi, body, 0)

    def pipeline(stages, hooks):
        cuts = set(hooks)
        for _, offset, size in stages:
            cuts |= {offset, offset + size}
        cuts = sorted(cuts)
        for lo, hi in zip(cuts, cuts[1:] + cuts[-1:]):
            for act in hooks.get(lo, ()):
                act()
            active = [(body, offset) for body, offset, size in stages if offset <= lo and hi <= offset + size]
            if lo < hi and active:
                loop(lo, hi, *[lambda i, body=body, offset=offset: body(i - offset) for body, offset in active])

    def settle(is_early, k):
        pair_link(k).wait_recv()
        near_link(k).wait_recv()

        def put(f, j, x, value):
            value = value + (pair_r[k, f, j] + near_r[k, f, j])
            if f < 2:
                fld0[f, j, x] = value
            else:
                mob[j, x] = value
        held(is_early, k, me, put)

    def ghost_link(t, side):
        return pltpu.make_async_remote_copy(
            src_ref=flds[t].at[:, :, 0 if side else EDGE - 1], dst_ref=ghosts[t].at[side],
            send_sem=hs.at[t, side], recv_sem=hr.at[t, side],
            device_id=(down if side else up,), device_id_type=pl.DeviceIdType.MESH)

    def start_ghosts(t):
        pl.when(has_up)(lambda: ghost_link(t, 0).start())
        pl.when(has_down)(lambda: ghost_link(t, 1).start())

    def await_ghosts(t):
        pl.when(has_down)(lambda: ghost_link(t, 0).wait_recv())
        pl.when(has_up)(lambda: ghost_link(t, 1).wait_recv())

    def await_sent(t):
        pl.when(has_up)(lambda: ghost_link(t, 0).wait_send())
        pl.when(has_down)(lambda: ghost_link(t, 1).wait_send())

    local, advance, keep, middle = stepper(cap, nbs, flds, mob, phi_out, conc_out, 0)

    def ends(t):
        fld, ghost, last = flds[t], ghosts[t], EDGE - 1
        await_ghosts(t)
        results = []
        for b in range(cap):
            at_x0, has_x0 = local(0, b)
            at_x1, has_x1 = local(1, b)
            results.append((b, 0, advance(t, b, 0, lambda f: (
                jnp.where(has_x0, ghost[0, f, at_x0], fld[f, b, 0]), fld[f, b, 1]))))
            results.append((b, last, advance(t, b, last, lambda f: (
                fld[f, b, last - 1], jnp.where(has_x1, ghost[1, f, at_x1], fld[f, b, last])))))
        for b, x, result in results:
            keep(t, b, x, *result)
        if t + 1 < STEPS:
            start_ghosts(t + 1)

    for copy in early_loads:
        copy.wait()
    pl.semaphore_wait(barrier, expected)
    near_at = AHEAD + LAG
    settle_at = near_at + SETTLE
    stages = []
    for body, offset in ((send_side, 0), (send_far, AHEAD), (send_near, near_at), (send_pair, near_at), (settle, settle_at)):
        stages.append((functools.partial(body, True), offset, EARLY))
        stages.append((lambda i, body=body: body(False, i + EARLY), offset + EARLY, EDGE - EARLY))

    def await_late():
        for copy in late_loads:
            copy.wait()

    hooks = {EARLY: (await_late,)}
    hooks[settle_at + 2] = hooks.get(settle_at + 2, ()) + (lambda: start_ghosts(0),)
    for t in range(STEPS):
        begin = settle_at + 2 + SLACK * t
        doubles = max(SLACK * t - lag(t), 0)
        if doubles:
            def two(i, t=t):
                middle(t, 2 * i + 2)
                middle(t, 2 * i + 3)
            stages.append((two, begin, doubles))
        done = 2 + 2 * doubles
        stages.append((lambda i, t=t, done=done: middle(t, i + done), settle_at + done + lag(t), EDGE - lag(t) - done))
        hooks[begin + SLACK] = hooks.get(begin + SLACK, ()) + (functools.partial(ends, t),)
    pipeline(stages, hooks)

    def sent(k):
        side_link(k).wait_send()
        pair_link(k).wait_send()
        pl.when(sends_far)(lambda: far_link(k).wait_send())
        near_link(k).wait_send()

    loop(0, EDGE, sent)
    for t in range(STEPS):
        await_sent(t)


class Patched:
    def __init__(self, field, patch, first, size):
        self.field, self.patch, self.first, self.size = field, patch, first, size

    def __getitem__(self, at):
        f, b, x = at
        if self.first <= x < self.first + self.size:
            return self.patch[f, b, x - self.first]
        return self.field[f, b, x]

    def __setitem__(self, at, value):
        f, b, x = at
        self.patch[f, b, x - self.first] = value


def finish(cap, nbs, phi_ref, conc_ref, fld0, fld1, fld2, mob, phi_out, conc_out,
           new1, new2, phi_last, conc_last, sem):
    size = lag(STEPS - 1)
    first, sheet = (EDGE - size) // 2, SUB * SUB
    early, late = [], []
    for i, (ref, last, out) in enumerate(((phi_ref, phi_last, phi_out), (conc_ref, conc_last, conc_out))):
        for q in range(cap // SUB):
            for side, (lo, hi) in enumerate(((0, first), (first + size, EDGE))):
                at = pl.ds((q * EDGE + lo) * sheet, (hi - lo) * sheet)
                early.append(pltpu.make_async_copy(ref.at[at], out.at[at], sem.at[i, q, side]))
            late.append(pltpu.make_async_copy(
                last.at[pl.ds(q * size * sheet, size * sheet)],
                out.at[pl.ds((q * EDGE + first) * sheet, size * sheet)], sem.at[i, q, 2]))
    for copy in early:
        copy.start()
    flds = [fld0]
    for t, (field, patch) in enumerate(((fld1, new1), (fld2, new2))):
        flds.append(Patched(field, patch, (EDGE - lag(t)) // 2, lag(t)))
    *_, middle = stepper(cap, nbs, flds, mob, phi_last, conc_last, first)
    for t in range(STEPS):
        for k in range(EDGE - lag(t), EDGE):
            middle(t, k)
    for copy in late:
        copy.start()
    for copy in early + late:
        copy.wait()


def on_device(n, old_phase, old_solute, old_mobility, new_global_slot, neighbors):
    cap = neighbors.shape[0]
    nold, cells = old_phase.shape
    rows = cells // LANES

    def tiled(field):
        split = field.reshape(nold // SUB, SUB, rows, LANES)
        return split.transpose(0, 2, 1, 3).reshape(nold * rows, LANES)

    def flat(field):
        split = field.reshape(cap // SUB, rows, SUB, LANES)
        return split.transpose(0, 2, 1, 3).reshape(cap, cells)

    def vmem(*shape):
        return pltpu.VMEM(shape, jnp.float32)

    in_vmem, anywhere = pl.BlockSpec(memory_space=pltpu.VMEM), pl.BlockSpec(memory_space=pl.ANY)
    in_smem = pl.BlockSpec(memory_space=pltpu.SMEM)
    field = vmem(2, cap, EDGE, SUB, LANES)
    buffer = vmem(EDGE, FIELDS, cap, SUB, LANES)
    tiles, sheet = nold // SUB, SUB * SUB
    state = pl.pallas_call(
        functools.partial(kernel, n, cap, nold),
        out_shape=(vmem(cap * rows, LANES),) * 2 + (field,) * STEPS + (vmem(cap, EDGE, SUB, LANES),),
        in_specs=[in_smem] * 2 + [anywhere] * 3,
        out_specs=[in_vmem] * (3 + STEPS),
        scratch_shapes=[vmem(FIELDS * tiles * EARLY * sheet, LANES), vmem(FIELDS * tiles * (EDGE - EARLY) * sheet, LANES)]
        + [buffer] * 8 + [vmem(2, 2, cap, SUB, LANES)] * STEPS + [
            pltpu.SemaphoreType.DMA((FIELDS, tiles, 2)),
            pltpu.SemaphoreType.DMA((FIELDS, tiles)),
            pltpu.SemaphoreType.DMA((4, EDGE)),
            pltpu.SemaphoreType.DMA((4, EDGE)),
            pltpu.SemaphoreType.DMA((STEPS, 2)),
            pltpu.SemaphoreType.DMA((STEPS, 2)),
        ],
        compiler_params=pltpu.CompilerParams(
            collective_id=0, has_side_effects=True, vmem_limit_bytes=44 * 1024 * 1024),
    )(*[pltpu.with_memory_space_constraint(table, pltpu.HBM) for table in (new_global_slot, neighbors)], tiled(old_phase), tiled(old_solute), tiled(old_mobility))
    last = vmem(cap * lag(STEPS - 1) * SUB, LANES)
    phase, solute = pl.pallas_call(
        functools.partial(finish, cap),
        out_shape=(jax.ShapeDtypeStruct((cap * rows, LANES), jnp.float32),) * 2,
        in_specs=[in_smem] + [in_vmem] * (3 + STEPS),
        out_specs=[anywhere] * 2,
        scratch_shapes=[vmem(2, cap, lag(t), SUB, LANES) for t in range(STEPS - 1)] + [last] * 2 + [
            pltpu.SemaphoreType.DMA((2, cap // SUB, 3))],
        compiler_params=pltpu.CompilerParams(vmem_limit_bytes=32 * 1024 * 1024),
    )(neighbors, *[pltpu.with_memory_space_constraint(each, pltpu.VMEM) for each in state])
    return flat(phase), flat(solute)


def solution(mesh):
    placed = (P("blk", None), P("blk", None), P("blk", None), P("blk"), P("blk", None))
    return jax.shard_map(
        functools.partial(on_device, mesh.shape["blk"]),
        mesh=mesh,
        in_specs=placed,
        out_specs=(P("blk", None), P("blk", None)),
        check_vma=False,
    )
```

```python
import functools

import jax
import jax.numpy as jnp
from jax import lax
from jax.experimental import pallas as pl
from jax.experimental.pallas import tpu as pltpu
from jax.sharding import PartitionSpec as P

EDGE = 32
STEPS = 3
FIELDS = 3
SUB = 8
LANES = 128
AHEAD = 4
LAG = 3
SETTLE = 3
SLACK = 6
EARLY = 8
FIRST, LATE, CENTER = range(3)

time_step = 0.15
coupling = 1.5


def plane(k):
    half = k // 2 if isinstance(k, int) else lax.div(k, 2)
    if isinstance(k, int):
        return EDGE - 1 - half if k % 2 else half
    return jnp.where(lax.rem(k, 2) == 0, half, EDGE - 1 - half)


def lag(t):
    return 2 * (t + 1)


def stepper(cap, nbs, flds, mob, phi_out, conc_out, first):
    lane = lax.broadcasted_iota(jnp.int32, (SUB, LANES), 1)
    row = lax.broadcasted_iota(jnp.int32, (SUB, LANES), 0)
    z = lane % EDGE
    z_low, z_high = z == 0, z == EDGE - 1
    y_first, y_last = lane < EDGE, lane >= LANES - EDGE
    y_start, y_end = y_first & (row == 0), y_last & (row == SUB - 1)

    def local(column, b):
        index = nbs[b, column]
        return lax.rem(jnp.maximum(index, 0), cap), index >= 0

    def advance(t, b, x, beside):
        fld = flds[t]
        at_y0, has_y0 = local(2, b)
        at_y1, has_y1 = local(3, b)
        at_z0, _ = local(4, b)
        at_z1, _ = local(5, b)
        wall_y0 = y_start & jnp.logical_not(has_y0)
        wall_y1 = y_end & jnp.logical_not(has_y1)

        def laplacian(f, here):
            prev_x, next_x = beside(f)
            y0, y1 = fld[f, at_y0, x], fld[f, at_y1, x]
            z0, z1 = fld[f, at_z0, x], fld[f, at_z1, x]
            back = pltpu.roll(jnp.where(y_end, y0, here), EDGE, 1)
            prev_y = jnp.where(y_first, pltpu.roll(back, 1, 0), back)
            prev_y = jnp.where(wall_y0, here, prev_y)
            fore = pltpu.roll(jnp.where(y_start, y1, here), LANES - EDGE, 1)
            next_y = jnp.where(y_last, pltpu.roll(fore, SUB - 1, 0), fore)
            next_y = jnp.where(wall_y1, here, next_y)
            prev_z = jnp.where(z_low, pltpu.roll(z0, LANES - (EDGE - 1), 1), pltpu.roll(here, 1, 1))
            next_z = jnp.where(z_high, pltpu.roll(z1, EDGE - 1, 1), pltpu.roll(here, LANES - 1, 1))
            return (prev_x + next_x) + (prev_y + next_y) + (prev_z + next_z) - 6.0 * here

        phi, conc = fld[0, b, x], fld[1, b, x]
        wetting = 1.0 - phi * phi
        drive = laplacian(0, phi) + phi - phi * phi * phi - coupling * conc * wetting * wetting
        new_phi = phi + time_step * mob[b, x] * drive
        new_conc = conc + time_step * laplacian(1, conc) + 0.5 * (new_phi - phi)
        return new_phi, new_conc

    def keep(t, b, x, new_phi, new_conc):
        if t == STEPS - 1:
            at = b % SUB + (x - first) * (SUB * SUB) + (b // SUB) * (phi_out.shape[0] // (cap // SUB))
            phi_out[pl.ds(at, SUB, stride=SUB), :] = new_phi
            conc_out[pl.ds(at, SUB, stride=SUB), :] = new_conc
        else:
            flds[t + 1][0, b, x] = new_phi
            flds[t + 1][1, b, x] = new_conc

    def middle(t, k):
        x = plane(k)
        fld = flds[t]
        results = [advance(t, b, x, lambda f, b=b: (fld[f, b, x - 1], fld[f, b, x + 1])) for b in range(cap)]
        for b, result in enumerate(results):
            keep(t, b, x, *result)

    return local, advance, keep, middle


def kernel(n, cap, nold, ngs_ref, nbs_ref, op, oc, om, phi_out, conc_out, fld0, fld1, fld2, mob, early, late, center,
           side_s, side_r, pair_s, pair_r, far_s, far_r, near_s, near_r,
           cross_r, direct_r, ghost0, ghost1, ghost2, ngs, nbs, tsem, xsem, esem, lsem, msem, ssem, rsem, hs, hr):
    flds = (fld0, fld1, fld2)
    ghosts = (ghost0, ghost1, ghost2)
    sheet = SUB * SUB
    tiles = nold // SUB
    edge, inside = EARLY // 2, EDGE - EARLY
    early_loads, late_loads = [], []
    for f, src in enumerate((op, oc, om)):
        for q in range(tiles):
            for side in range(2):
                at = q * EDGE + side * (EDGE - edge)
                early_loads.append(pltpu.make_async_copy(
                    src.at[pl.ds(at * sheet, edge * sheet)],
                    early.at[pl.ds(((f * tiles + q) * EARLY + side * edge) * sheet, edge * sheet)], esem.at[f, q, side]))
            late_loads.append(pltpu.make_async_copy(
                src.at[pl.ds((q * EDGE + edge) * sheet, inside * sheet)],
                late.at[pl.ds((f * tiles + q) * inside * sheet, inside * sheet)], lsem.at[f, q]))
            early_loads.append(pltpu.make_async_copy(
                src.at[pl.ds((q * EDGE + plane(EDGE - 1)) * sheet, sheet)],
                center.at[pl.ds((f * tiles + q) * sheet, sheet)], msem.at[f, q]))
    tables = [
        pltpu.make_async_copy(src, dst, tsem.at[i])
        for i, (src, dst) in enumerate(((ngs_ref, ngs), (nbs_ref, nbs)))
    ]
    for copy in tables + early_loads + late_loads:
        copy.start()

    me = lax.axis_index("blk")
    core = me % 2
    odd = (me // 2) % 2
    sib = me + 1 - 2 * core
    near = me + 2 - 4 * odd
    far_final = me - 2 + 4 * odd
    far = me - 4 + 8 * odd
    far_source = me + 4 - 8 * odd
    side_final = me - 1 + 2 * core
    up, down = me + 1, me - 1
    has_up, has_down = up < n, down >= 0
    sends_far = (far_final >= 0) & (far_final < n)
    gets_far = (far_source >= 0) & (far_source < n)

    barrier = pltpu.get_barrier_semaphore()
    expected = jnp.int32(0)
    for other, there in ((up, has_up), (down, has_down), (near, None), (far, sends_far), (far_source, gets_far)):
        def greet(other=other):
            pl.semaphore_signal(barrier, inc=1, device_id=(other,), device_id_type=pl.DeviceIdType.MESH)
        if there is None:
            greet()
            expected = expected + 1
        else:
            pl.when(there)(greet)
            expected = expected + there.astype(jnp.int32)

    for copy in tables:
        copy.wait()
    start = ngs[0]
    count = jnp.int32(0)
    for s in range(nold):
        count = count + (ngs[s] >= 0).astype(jnp.int32)

    def held(part, k, final, put):
        x = plane(k)
        if part == CENTER:
            source, held_planes, at_plane = center, 1, 0
        elif part == FIRST:
            source, held_planes, at_plane = early, EARLY, jnp.where(x < edge, x, x - inside)
        else:
            source, held_planes, at_plane = late, inside, x - edge
        for j in range(cap):
            idx = final * cap + j - start
            mine = (idx >= 0) & (idx < count)
            idx = jnp.clip(idx, 0, nold - 1)
            row = lax.div(idx, SUB) * (held_planes * sheet) + lax.rem(idx, SUB) + at_plane * sheet
            for f in range(FIELDS):
                got = source[pl.ds(f * (tiles * held_planes * sheet) + row, SUB, stride=SUB), :]
                put(f, j, x, jnp.where(mine, got, 0.0))

    def link(stream, src, dst, k, target):
        return pltpu.make_async_remote_copy(
            src_ref=src.at[k], dst_ref=dst.at[k],
            send_sem=ssem.at[stream, k], recv_sem=rsem.at[stream, k],
            device_id=(target,), device_id_type=pl.DeviceIdType.MESH)

    def side_link(k):
        return link(0, side_s, side_r, k, sib)

    def pair_link(k):
        return link(1, pair_s, pair_r, k, sib)

    def far_link(k):
        return link(2, far_s, far_r, k, far)

    def near_link(k):
        return link(3, near_s, near_r, k, near)

    side_goes_far = (core + odd) % 2 == 1

    def fill(part, buffer, k, final):
        def put(f, j, x, value):
            buffer[k, f, j] = value
        held(part, k, final, put)

    def send_side(part, k):
        fill(part, side_s, k, side_final)
        side_link(k).start()

    def send_pair(part, k):
        fill(part, pair_s, k, sib)
        pair_link(k).start()

    def cross_link():
        return pltpu.make_async_remote_copy(
            src_ref=far_s.at[EDGE - 1], dst_ref=cross_r, send_sem=xsem.at[0], recv_sem=xsem.at[1],
            device_id=(near,), device_id_type=pl.DeviceIdType.MESH)

    def direct_link():
        return pltpu.make_async_remote_copy(
            src_ref=cross_r, dst_ref=direct_r, send_sem=xsem.at[2], recv_sem=xsem.at[3],
            device_id=(far_source,), device_id_type=pl.DeviceIdType.MESH)

    def add_side(k, total):
        side_link(k).wait_recv()
        total[k] += side_r[k]

    def send_far(part, k):
        fill(part, far_s, k, far_final)
        pl.when(side_goes_far)(lambda: add_side(k, far_s))
        pl.when(sends_far)(lambda: far_link(k).start())

    def send_near(part, k):
        fill(part, near_s, k, near)
        pl.when(jnp.logical_not(side_goes_far))(lambda: add_side(k, near_s))

        @pl.when(gets_far)
        def add_far():
            far_link(k).wait_recv()
            near_s[k] += far_r[k]

        near_link(k).start()

    def send_center():
        k = EDGE - 1
        fill(CENTER, near_s, k, near)
        fill(CENTER, far_s, k, far_final)

        @pl.when(side_goes_far)
        def near_first():
            near_link(k).start()
            add_side(k, far_s)
            pl.when(sends_far)(lambda: cross_link().start())

        @pl.when(jnp.logical_not(side_goes_far))
        def far_first():
            pl.when(sends_far)(lambda: cross_link().start())
            add_side(k, near_s)
            near_link(k).start()

    def hand_on():
        @pl.when(gets_far)
        def pass_center():
            cross_link().wait_recv()
            direct_link().start()

    def loop(lo, hi, *bodies):
        def body(i, carry):
            for each in bodies:
                each(i)
            return carry
        lax.fori_loop(lo, hi, body, 0)

    def pipeline(stages, hooks):
        cuts = set(hooks)
        for _, offset, size in stages:
            cuts |= {offset, offset + size}
        cuts = sorted(cuts)
        for lo, hi in zip(cuts, cuts[1:] + cuts[-1:]):
            for act in hooks.get(lo, ()):
                act()
            active = [(body, offset) for body, offset, size in stages if offset <= lo and hi <= offset + size]
            if lo < hi and active:
                loop(lo, hi, *[lambda i, body=body, offset=offset: body(i - offset) for body, offset in active])

    def settle(part, k):
        pair_link(k).wait_recv()
        near_link(k).wait_recv()
        if part == CENTER:
            @pl.when(sends_far)
            def add_direct():
                direct_link().wait_recv()
                near_r[k] += direct_r[...]

        def put(f, j, x, value):
            value = value + (pair_r[k, f, j] + near_r[k, f, j])
            if f < 2:
                fld0[f, j, x] = value
            else:
                mob[j, x] = value
        held(part, k, me, put)

    def ghost_link(t, side):
        return pltpu.make_async_remote_copy(
            src_ref=flds[t].at[:, :, 0 if side else EDGE - 1], dst_ref=ghosts[t].at[side],
            send_sem=hs.at[t, side], recv_sem=hr.at[t, side],
            device_id=(down if side else up,), device_id_type=pl.DeviceIdType.MESH)

    def start_ghosts(t):
        pl.when(has_up)(lambda: ghost_link(t, 0).start())
        pl.when(has_down)(lambda: ghost_link(t, 1).start())

    def await_ghosts(t):
        pl.when(has_down)(lambda: ghost_link(t, 0).wait_recv())
        pl.when(has_up)(lambda: ghost_link(t, 1).wait_recv())

    def await_sent(t):
        pl.when(has_up)(lambda: ghost_link(t, 0).wait_send())
        pl.when(has_down)(lambda: ghost_link(t, 1).wait_send())

    local, advance, keep, middle = stepper(cap, nbs, flds, mob, phi_out, conc_out, 0)

    def ends(t):
        fld, ghost, last = flds[t], ghosts[t], EDGE - 1
        await_ghosts(t)
        results = []
        for b in range(cap):
            at_x0, has_x0 = local(0, b)
            at_x1, has_x1 = local(1, b)
            results.append((b, 0, advance(t, b, 0, lambda f: (
                jnp.where(has_x0, ghost[0, f, at_x0], fld[f, b, 0]), fld[f, b, 1]))))
            results.append((b, last, advance(t, b, last, lambda f: (
                fld[f, b, last - 1], jnp.where(has_x1, ghost[1, f, at_x1], fld[f, b, last])))))
        for b, x, result in results:
            keep(t, b, x, *result)
        if t + 1 < STEPS:
            start_ghosts(t + 1)

    for copy in early_loads:
        copy.wait()
    pl.semaphore_wait(barrier, expected)
    near_at = AHEAD + LAG
    settle_at = near_at + SETTLE
    stages = []
    for body, offset in ((send_side, 0), (send_far, AHEAD), (send_near, near_at), (send_pair, near_at), (settle, settle_at)):
        stages.append((functools.partial(body, FIRST), offset, EARLY))
        size = EDGE if body is send_pair else EDGE - 1
        stages.append((lambda i, body=body: body(LATE, i + EARLY), offset + EARLY, size - EARLY))
    stages.append((lambda i: settle(CENTER, EDGE - 1), settle_at + EDGE - 1, 1))

    def await_late():
        for copy in late_loads:
            copy.wait()

    hooks = {
        0: (functools.partial(send_side, CENTER, EDGE - 1),),
        AHEAD + 1: (send_center,),
        EARLY: (await_late,),
        AHEAD + EDGE - 1: (hand_on,),
    }
    hooks[settle_at + 2] = hooks.get(settle_at + 2, ()) + (lambda: start_ghosts(0),)
    for t in range(STEPS):
        begin = settle_at + 2 + SLACK * t
        doubles = max(SLACK * t - lag(t), 0)
        if doubles:
            def two(i, t=t):
                middle(t, 2 * i + 2)
                middle(t, 2 * i + 3)
            stages.append((two, begin, doubles))
        done = 2 + 2 * doubles
        stages.append((lambda i, t=t, done=done: middle(t, i + done), settle_at + done + lag(t), EDGE - lag(t) - done))
        hooks[begin + SLACK] = hooks.get(begin + SLACK, ()) + (functools.partial(ends, t),)
    pipeline(stages, hooks)

    def sent(k):
        side_link(k).wait_send()
        pair_link(k).wait_send()
        near_link(k).wait_send()

    def far_sent(k):
        far_link(k).wait_send()

    loop(0, EDGE, sent)

    @pl.when(sends_far)
    def await_far_sent():
        loop(0, EDGE - 1, far_sent)
        cross_link().wait_send()

    pl.when(gets_far)(lambda: direct_link().wait_send())
    for t in range(STEPS):
        await_sent(t)


class Patched:
    def __init__(self, field, patch, first, size):
        self.field, self.patch, self.first, self.size = field, patch, first, size

    def __getitem__(self, at):
        f, b, x = at
        if self.first <= x < self.first + self.size:
            return self.patch[f, b, x - self.first]
        return self.field[f, b, x]

    def __setitem__(self, at, value):
        f, b, x = at
        self.patch[f, b, x - self.first] = value


def finish(cap, nbs, phi_ref, conc_ref, fld0, fld1, fld2, mob, phi_out, conc_out,
           new1, new2, phi_last, conc_last, sem):
    size = lag(STEPS - 1)
    first, sheet = (EDGE - size) // 2, SUB * SUB
    early, late = [], []
    for i, (ref, last, out) in enumerate(((phi_ref, phi_last, phi_out), (conc_ref, conc_last, conc_out))):
        for q in range(cap // SUB):
            for side, (lo, hi) in enumerate(((0, first), (first + size, EDGE))):
                at = pl.ds((q * EDGE + lo) * sheet, (hi - lo) * sheet)
                early.append(pltpu.make_async_copy(ref.at[at], out.at[at], sem.at[i, q, side]))
            late.append(pltpu.make_async_copy(
                last.at[pl.ds(q * size * sheet, size * sheet)],
                out.at[pl.ds((q * EDGE + first) * sheet, size * sheet)], sem.at[i, q, 2]))
    for copy in early:
        copy.start()
    flds = [fld0]
    for t, (field, patch) in enumerate(((fld1, new1), (fld2, new2))):
        flds.append(Patched(field, patch, (EDGE - lag(t)) // 2, lag(t)))
    *_, middle = stepper(cap, nbs, flds, mob, phi_last, conc_last, first)
    for t in range(STEPS):
        for k in range(EDGE - lag(t), EDGE):
            middle(t, k)
    for copy in late:
        copy.start()
    for copy in early + late:
        copy.wait()


def on_device(n, old_phase, old_solute, old_mobility, new_global_slot, neighbors):
    cap = neighbors.shape[0]
    nold, cells = old_phase.shape
    rows = cells // LANES

    def tiled(field):
        split = field.reshape(nold // SUB, SUB, rows, LANES)
        return split.transpose(0, 2, 1, 3).reshape(nold * rows, LANES)

    def flat(field):
        split = field.reshape(cap // SUB, rows, SUB, LANES)
        return split.transpose(0, 2, 1, 3).reshape(cap, cells)

    def vmem(*shape):
        return pltpu.VMEM(shape, jnp.float32)

    in_vmem, anywhere = pl.BlockSpec(memory_space=pltpu.VMEM), pl.BlockSpec(memory_space=pl.ANY)
    in_smem = pl.BlockSpec(memory_space=pltpu.SMEM)
    field = vmem(2, cap, EDGE, SUB, LANES)
    buffer = vmem(EDGE, FIELDS, cap, SUB, LANES)
    tiles, sheet = nold // SUB, SUB * SUB
    state = pl.pallas_call(
        functools.partial(kernel, n, cap, nold),
        out_shape=(vmem(cap * rows, LANES),) * 2 + (field,) * STEPS + (vmem(cap, EDGE, SUB, LANES),),
        in_specs=[anywhere] * 5,
        out_specs=[in_vmem] * (3 + STEPS),
        scratch_shapes=[vmem(FIELDS * tiles * EARLY * sheet, LANES), vmem(FIELDS * tiles * (EDGE - EARLY) * sheet, LANES)]
        + [vmem(FIELDS * tiles * sheet, LANES)] + [buffer] * 8 + [vmem(FIELDS, cap, SUB, LANES)] * 2 + [vmem(2, 2, cap, SUB, LANES)] * STEPS + [
            pltpu.SMEM(new_global_slot.shape, jnp.int32),
            pltpu.SMEM(neighbors.shape, jnp.int32),
            pltpu.SemaphoreType.DMA((2,)),
            pltpu.SemaphoreType.DMA((4,)),
            pltpu.SemaphoreType.DMA((FIELDS, tiles, 2)),
            pltpu.SemaphoreType.DMA((FIELDS, tiles)),
            pltpu.SemaphoreType.DMA((FIELDS, tiles)),
            pltpu.SemaphoreType.DMA((4, EDGE)),
            pltpu.SemaphoreType.DMA((4, EDGE)),
            pltpu.SemaphoreType.DMA((STEPS, 2)),
            pltpu.SemaphoreType.DMA((STEPS, 2)),
        ],
        compiler_params=pltpu.CompilerParams(
            collective_id=0, has_side_effects=True, vmem_limit_bytes=44 * 1024 * 1024),
    )(*[pltpu.with_memory_space_constraint(table, pltpu.HBM) for table in (new_global_slot, neighbors)], tiled(old_phase), tiled(old_solute), tiled(old_mobility))
    last = vmem(cap * lag(STEPS - 1) * SUB, LANES)
    phase, solute = pl.pallas_call(
        functools.partial(finish, cap),
        out_shape=(jax.ShapeDtypeStruct((cap * rows, LANES), jnp.float32),) * 2,
        in_specs=[in_smem] + [in_vmem] * (3 + STEPS),
        out_specs=[anywhere] * 2,
        scratch_shapes=[vmem(2, cap, lag(t), SUB, LANES) for t in range(STEPS - 1)] + [last] * 2 + [
            pltpu.SemaphoreType.DMA((2, cap // SUB, 3))],
        compiler_params=pltpu.CompilerParams(vmem_limit_bytes=32 * 1024 * 1024),
    )(neighbors, *[pltpu.with_memory_space_constraint(each, pltpu.VMEM) for each in state])
    return flat(phase), flat(solute)


def solution(mesh):
    placed = (P("blk", None), P("blk", None), P("blk", None), P("blk"), P("blk", None))
    return jax.shard_map(
        functools.partial(on_device, mesh.shape["blk"]),
        mesh=mesh,
        in_specs=placed,
        out_specs=(P("blk", None), P("blk", None)),
        check_vma=False,
    )
```

```python
import functools

import jax
import jax.numpy as jnp
from jax import lax
from jax.experimental import pallas as pl
from jax.experimental.pallas import tpu as pltpu
from jax.sharding import PartitionSpec as P

EDGE = 32
STEPS = 3
FIELDS = 3
SUB = 8
LANES = 128
AHEAD = 4
LAG = 3
SETTLE = 2
SLACK = 6
EARLY = 4
FIRST, LATE, CENTER = range(3)

time_step = 0.15
coupling = 1.5


def plane(k):
    half = k // 2 if isinstance(k, int) else lax.div(k, 2)
    if isinstance(k, int):
        return EDGE - 1 - half if k % 2 else half
    return jnp.where(lax.rem(k, 2) == 0, half, EDGE - 1 - half)


def lag(t):
    return 2 * (t + 1)


def stepper(cap, nbs, flds, mob, phi_out, conc_out, first):
    lane = lax.broadcasted_iota(jnp.int32, (SUB, LANES), 1)
    row = lax.broadcasted_iota(jnp.int32, (SUB, LANES), 0)
    z = lane % EDGE
    z_low, z_high = z == 0, z == EDGE - 1
    y_first, y_last = lane < EDGE, lane >= LANES - EDGE
    y_start, y_end = y_first & (row == 0), y_last & (row == SUB - 1)

    def local(column, b):
        index = nbs[b, column]
        return lax.rem(jnp.maximum(index, 0), cap), index >= 0

    def advance(t, b, x, beside):
        fld = flds[t]
        at_y0, has_y0 = local(2, b)
        at_y1, has_y1 = local(3, b)
        at_z0, _ = local(4, b)
        at_z1, _ = local(5, b)
        wall_y0 = y_start & jnp.logical_not(has_y0)
        wall_y1 = y_end & jnp.logical_not(has_y1)

        def laplacian(f, here):
            prev_x, next_x = beside(f)
            y0, y1 = fld[f, at_y0, x], fld[f, at_y1, x]
            z0, z1 = fld[f, at_z0, x], fld[f, at_z1, x]
            back = pltpu.roll(jnp.where(y_end, y0, here), EDGE, 1)
            prev_y = jnp.where(y_first, pltpu.roll(back, 1, 0), back)
            prev_y = jnp.where(wall_y0, here, prev_y)
            fore = pltpu.roll(jnp.where(y_start, y1, here), LANES - EDGE, 1)
            next_y = jnp.where(y_last, pltpu.roll(fore, SUB - 1, 0), fore)
            next_y = jnp.where(wall_y1, here, next_y)
            prev_z = jnp.where(z_low, pltpu.roll(z0, LANES - (EDGE - 1), 1), pltpu.roll(here, 1, 1))
            next_z = jnp.where(z_high, pltpu.roll(z1, EDGE - 1, 1), pltpu.roll(here, LANES - 1, 1))
            return (prev_x + next_x) + (prev_y + next_y) + (prev_z + next_z) - 6.0 * here

        phi, conc = fld[0, b, x], fld[1, b, x]
        wetting = 1.0 - phi * phi
        drive = laplacian(0, phi) + phi - phi * phi * phi - coupling * conc * wetting * wetting
        new_phi = phi + time_step * mob[b, x] * drive
        new_conc = conc + time_step * laplacian(1, conc) + 0.5 * (new_phi - phi)
        return new_phi, new_conc

    def keep(t, b, x, new_phi, new_conc):
        if t == STEPS - 1:
            at = b % SUB + (x - first) * (SUB * SUB) + (b // SUB) * (phi_out.shape[0] // (cap // SUB))
            phi_out[pl.ds(at, SUB, stride=SUB), :] = new_phi
            conc_out[pl.ds(at, SUB, stride=SUB), :] = new_conc
        else:
            flds[t + 1][0, b, x] = new_phi
            flds[t + 1][1, b, x] = new_conc

    def middle(t, k):
        x = plane(k)
        fld = flds[t]
        results = [advance(t, b, x, lambda f, b=b: (fld[f, b, x - 1], fld[f, b, x + 1])) for b in range(cap)]
        for b, result in enumerate(results):
            keep(t, b, x, *result)

    return local, advance, keep, middle


def kernel(n, cap, nold, ngs_ref, nbs_ref, op, oc, om, phi_out, conc_out, fld0, fld1, fld2, mob, early, late, center,
           side_s, side_r, pair_s, pair_r, far_s, far_r, near_s, near_r,
           cross_r, direct_r, ghost0, ghost1, ghost2, ngs, nbs, tsem, xsem, esem, lsem, msem, ssem, rsem, hs, hr):
    flds = (fld0, fld1, fld2)
    ghosts = (ghost0, ghost1, ghost2)
    sheet = SUB * SUB
    tiles = nold // SUB
    edge, inside = EARLY // 2, EDGE - EARLY
    early_loads, late_loads = [], []
    for f, src in enumerate((op, oc, om)):
        for q in range(tiles):
            for side in range(2):
                at = q * EDGE + side * (EDGE - edge)
                early_loads.append(pltpu.make_async_copy(
                    src.at[pl.ds(at * sheet, edge * sheet)],
                    early.at[pl.ds(((f * tiles + q) * EARLY + side * edge) * sheet, edge * sheet)], esem.at[f, q, side]))
            late_loads.append(pltpu.make_async_copy(
                src.at[pl.ds((q * EDGE + edge) * sheet, inside * sheet)],
                late.at[pl.ds((f * tiles + q) * inside * sheet, inside * sheet)], lsem.at[f, q]))
            early_loads.append(pltpu.make_async_copy(
                src.at[pl.ds((q * EDGE + plane(EDGE - 1)) * sheet, sheet)],
                center.at[pl.ds((f * tiles + q) * sheet, sheet)], msem.at[f, q]))
    tables = [
        pltpu.make_async_copy(src, dst, tsem.at[i])
        for i, (src, dst) in enumerate(((ngs_ref, ngs), (nbs_ref, nbs)))
    ]
    for copy in tables + early_loads + late_loads:
        copy.start()

    me = lax.axis_index("blk")
    core = me % 2
    odd = (me // 2) % 2
    sib = me + 1 - 2 * core
    near = me + 2 - 4 * odd
    far_final = me - 2 + 4 * odd
    far = me - 4 + 8 * odd
    far_source = me + 4 - 8 * odd
    side_final = me - 1 + 2 * core
    up, down = me + 1, me - 1
    has_up, has_down = up < n, down >= 0
    sends_far = (far_final >= 0) & (far_final < n)
    gets_far = (far_source >= 0) & (far_source < n)

    barrier = pltpu.get_barrier_semaphore()
    expected = jnp.int32(0)
    for other, there in ((up, has_up), (down, has_down), (near, None), (far, sends_far), (far_source, gets_far)):
        def greet(other=other):
            pl.semaphore_signal(barrier, inc=1, device_id=(other,), device_id_type=pl.DeviceIdType.MESH)
        if there is None:
            greet()
            expected = expected + 1
        else:
            pl.when(there)(greet)
            expected = expected + there.astype(jnp.int32)

    for copy in tables:
        copy.wait()
    start = ngs[0]
    count = jnp.int32(0)
    for s in range(nold):
        count = count + (ngs[s] >= 0).astype(jnp.int32)

    def held(part, k, final, put):
        x = plane(k)
        if part == CENTER:
            source, held_planes, at_plane = center, 1, 0
        elif part == FIRST:
            source, held_planes, at_plane = early, EARLY, jnp.where(x < edge, x, x - inside)
        else:
            source, held_planes, at_plane = late, inside, x - edge
        for j in range(cap):
            idx = final * cap + j - start
            mine = (idx >= 0) & (idx < count)
            idx = jnp.clip(idx, 0, nold - 1)
            row = lax.div(idx, SUB) * (held_planes * sheet) + lax.rem(idx, SUB) + at_plane * sheet
            for f in range(FIELDS):
                got = source[pl.ds(f * (tiles * held_planes * sheet) + row, SUB, stride=SUB), :]
                put(f, j, x, jnp.where(mine, got, 0.0))

    def link(stream, src, dst, k, target):
        return pltpu.make_async_remote_copy(
            src_ref=src.at[k], dst_ref=dst.at[k],
            send_sem=ssem.at[stream, k], recv_sem=rsem.at[stream, k],
            device_id=(target,), device_id_type=pl.DeviceIdType.MESH)

    def side_link(k):
        return link(0, side_s, side_r, k, sib)

    def pair_link(k):
        return link(1, pair_s, pair_r, k, sib)

    def far_link(k):
        return link(2, far_s, far_r, k, far)

    def near_link(k):
        return link(3, near_s, near_r, k, near)

    side_goes_far = (core + odd) % 2 == 1

    def fill(part, buffer, k, final):
        def put(f, j, x, value):
            buffer[k, f, j] = value
        held(part, k, final, put)

    def send_side(part, k):
        fill(part, side_s, k, side_final)
        side_link(k).start()

    def send_pair(part, k):
        fill(part, pair_s, k, sib)
        pair_link(k).start()

    def cross_link():
        return pltpu.make_async_remote_copy(
            src_ref=far_s.at[EDGE - 1], dst_ref=cross_r, send_sem=xsem.at[0], recv_sem=xsem.at[1],
            device_id=(near,), device_id_type=pl.DeviceIdType.MESH)

    def direct_link():
        return pltpu.make_async_remote_copy(
            src_ref=cross_r, dst_ref=direct_r, send_sem=xsem.at[2], recv_sem=xsem.at[3],
            device_id=(far_source,), device_id_type=pl.DeviceIdType.MESH)

    def add_side(k, total):
        side_link(k).wait_recv()
        total[k] += side_r[k]

    def send_far(part, k):
        fill(part, far_s, k, far_final)
        pl.when(side_goes_far)(lambda: add_side(k, far_s))
        pl.when(sends_far)(lambda: far_link(k).start())

    def send_near(part, k):
        fill(part, near_s, k, near)
        pl.when(jnp.logical_not(side_goes_far))(lambda: add_side(k, near_s))

        @pl.when(gets_far)
        def add_far():
            far_link(k).wait_recv()
            near_s[k] += far_r[k]

        near_link(k).start()

    def send_center():
        k = EDGE - 1
        fill(CENTER, near_s, k, near)
        fill(CENTER, far_s, k, far_final)

        @pl.when(side_goes_far)
        def near_first():
            near_link(k).start()
            add_side(k, far_s)
            pl.when(sends_far)(lambda: cross_link().start())

        @pl.when(jnp.logical_not(side_goes_far))
        def far_first():
            pl.when(sends_far)(lambda: cross_link().start())
            add_side(k, near_s)
            near_link(k).start()

    def hand_on():
        @pl.when(gets_far)
        def pass_center():
            cross_link().wait_recv()
            direct_link().start()

    def loop(lo, hi, *bodies):
        def body(i, carry):
            for each in bodies:
                each(i)
            return carry
        lax.fori_loop(lo, hi, body, 0)

    def pipeline(stages, hooks):
        cuts = set(hooks)
        for _, offset, size in stages:
            cuts |= {offset, offset + size}
        cuts = sorted(cuts)
        for lo, hi in zip(cuts, cuts[1:] + cuts[-1:]):
            for act in hooks.get(lo, ()):
                act()
            active = [(body, offset) for body, offset, size in stages if offset <= lo and hi <= offset + size]
            if lo < hi and active:
                loop(lo, hi, *[lambda i, body=body, offset=offset: body(i - offset) for body, offset in active])

    def settle(part, k):
        pair_link(k).wait_recv()
        near_link(k).wait_recv()
        if part == CENTER:
            @pl.when(sends_far)
            def add_direct():
                direct_link().wait_recv()
                near_r[k] += direct_r[...]

        def put(f, j, x, value):
            value = value + (pair_r[k, f, j] + near_r[k, f, j])
            if f < 2:
                fld0[f, j, x] = value
            else:
                mob[j, x] = value
        held(part, k, me, put)

    def sent(k):
        side_link(k).wait_send()
        pair_link(k).wait_send()
        near_link(k).wait_send()
        pl.when(sends_far)(lambda: far_link(k).wait_send())

    def ghost_link(t, side):
        return pltpu.make_async_remote_copy(
            src_ref=flds[t].at[:, :, 0 if side else EDGE - 1], dst_ref=ghosts[t].at[side],
            send_sem=hs.at[t, side], recv_sem=hr.at[t, side],
            device_id=(down if side else up,), device_id_type=pl.DeviceIdType.MESH)

    def start_ghosts(t):
        pl.when(has_up)(lambda: ghost_link(t, 0).start())
        pl.when(has_down)(lambda: ghost_link(t, 1).start())

    def await_ghosts(t):
        pl.when(has_down)(lambda: ghost_link(t, 0).wait_recv())
        pl.when(has_up)(lambda: ghost_link(t, 1).wait_recv())

    def await_sent(t):
        pl.when(has_up)(lambda: ghost_link(t, 0).wait_send())
        pl.when(has_down)(lambda: ghost_link(t, 1).wait_send())

    local, advance, keep, middle = stepper(cap, nbs, flds, mob, phi_out, conc_out, 0)

    def ends(t):
        fld, ghost, last = flds[t], ghosts[t], EDGE - 1
        await_ghosts(t)
        results = []
        for b in range(cap):
            at_x0, has_x0 = local(0, b)
            at_x1, has_x1 = local(1, b)
            results.append((b, 0, advance(t, b, 0, lambda f: (
                jnp.where(has_x0, ghost[0, f, at_x0], fld[f, b, 0]), fld[f, b, 1]))))
            results.append((b, last, advance(t, b, last, lambda f: (
                fld[f, b, last - 1], jnp.where(has_x1, ghost[1, f, at_x1], fld[f, b, last])))))
        for b, x, result in results:
            keep(t, b, x, *result)
        if t + 1 < STEPS:
            start_ghosts(t + 1)

    for copy in early_loads:
        copy.wait()
    pl.semaphore_wait(barrier, expected)
    near_at = AHEAD + LAG
    settle_at = near_at + SETTLE
    stages = []
    for body, offset in ((send_side, 0), (send_far, AHEAD), (send_near, near_at), (send_pair, near_at), (settle, settle_at)):
        stages.append((functools.partial(body, FIRST), offset, EARLY))
        size = EDGE if body is send_pair else EDGE - 1
        stages.append((lambda i, body=body: body(LATE, i + EARLY), offset + EARLY, size - EARLY))
    stages.append((lambda i: settle(CENTER, EDGE - 1), settle_at + EDGE - 1, 1))

    stages.append((sent, settle_at + 2, EDGE - 2))

    def await_late():
        for copy in late_loads:
            copy.wait()

    hooks = {
        0: (functools.partial(send_side, CENTER, EDGE - 1),),
        AHEAD + 1: (send_center,),
        EARLY: (await_late,),
        AHEAD + EDGE - 1: (hand_on,),
    }
    hooks[settle_at + 2] = hooks.get(settle_at + 2, ()) + (lambda: start_ghosts(0),)
    for t in range(STEPS):
        begin = settle_at + 2 + SLACK * t
        doubles = max(SLACK * t - lag(t), 0)
        if doubles:
            def two(i, t=t):
                middle(t, 2 * i + 2)
                middle(t, 2 * i + 3)
            stages.append((two, begin, doubles))
        done = 2 + 2 * doubles
        stages.append((lambda i, t=t, done=done: middle(t, i + done), settle_at + done + lag(t), EDGE - lag(t) - done))
        hooks[begin + SLACK] = hooks.get(begin + SLACK, ()) + (functools.partial(ends, t),)
    pipeline(stages, hooks)

    sent(EDGE - 2)
    for copy in (side_link(EDGE - 1), pair_link(EDGE - 1), near_link(EDGE - 1)):
        copy.wait_send()
    pl.when(sends_far)(lambda: cross_link().wait_send())
    pl.when(gets_far)(lambda: direct_link().wait_send())
    for t in range(STEPS):
        await_sent(t)


class Patched:
    def __init__(self, field, patch, first, size):
        self.field, self.patch, self.first, self.size = field, patch, first, size

    def __getitem__(self, at):
        f, b, x = at
        if self.first <= x < self.first + self.size:
            return self.patch[f, b, x - self.first]
        return self.field[f, b, x]

    def __setitem__(self, at, value):
        f, b, x = at
        self.patch[f, b, x - self.first] = value


def finish(cap, nbs, phi_ref, conc_ref, fld0, fld1, fld2, mob, phi_out, conc_out,
           new1, new2, phi_last, conc_last, sem):
    size = lag(STEPS - 1)
    first, sheet = (EDGE - size) // 2, SUB * SUB
    early, late = [], []
    for i, (ref, last, out) in enumerate(((phi_ref, phi_last, phi_out), (conc_ref, conc_last, conc_out))):
        for q in range(cap // SUB):
            for side, (lo, hi) in enumerate(((0, first), (first + size, EDGE))):
                at = pl.ds((q * EDGE + lo) * sheet, (hi - lo) * sheet)
                early.append(pltpu.make_async_copy(ref.at[at], out.at[at], sem.at[i, q, side]))
            for x in range(size):
                late.append((x, pltpu.make_async_copy(
                    last.at[pl.ds((q * size + x) * sheet, sheet)],
                    out.at[pl.ds((q * EDGE + first + x) * sheet, sheet)], sem.at[i, q, 2 + x])))
    for copy in early:
        copy.start()
    flds = [fld0]
    for t, (field, patch) in enumerate(((fld1, new1), (fld2, new2))):
        flds.append(Patched(field, patch, (EDGE - lag(t)) // 2, lag(t)))
    *_, middle = stepper(cap, nbs, flds, mob, phi_last, conc_last, first)
    for t in range(STEPS):
        for k in range(EDGE - lag(t), EDGE):
            middle(t, k)
            for x, copy in late:
                if t == STEPS - 1 and first + x == plane(k):
                    copy.start()
    for copy in early + [copy for _, copy in late]:
        copy.wait()


def on_device(n, old_phase, old_solute, old_mobility, new_global_slot, neighbors):
    cap = neighbors.shape[0]
    nold, cells = old_phase.shape
    rows = cells // LANES

    def tiled(field):
        split = field.reshape(nold // SUB, SUB, rows, LANES)
        return split.transpose(0, 2, 1, 3).reshape(nold * rows, LANES)

    def flat(field):
        split = field.reshape(cap // SUB, rows, SUB, LANES)
        return split.transpose(0, 2, 1, 3).reshape(cap, cells)

    def vmem(*shape):
        return pltpu.VMEM(shape, jnp.float32)

    in_vmem, anywhere = pl.BlockSpec(memory_space=pltpu.VMEM), pl.BlockSpec(memory_space=pl.ANY)
    in_smem = pl.BlockSpec(memory_space=pltpu.SMEM)
    field = vmem(2, cap, EDGE, SUB, LANES)
    buffer = vmem(EDGE, FIELDS, cap, SUB, LANES)
    tiles, sheet = nold // SUB, SUB * SUB
    state = pl.pallas_call(
        functools.partial(kernel, n, cap, nold),
        out_shape=(vmem(cap * rows, LANES),) * 2 + (field,) * STEPS + (vmem(cap, EDGE, SUB, LANES),),
        in_specs=[anywhere] * 5,
        out_specs=[in_vmem] * (3 + STEPS),
        scratch_shapes=[vmem(FIELDS * tiles * EARLY * sheet, LANES), vmem(FIELDS * tiles * (EDGE - EARLY) * sheet, LANES)]
        + [vmem(FIELDS * tiles * sheet, LANES)] + [buffer] * 8 + [vmem(FIELDS, cap, SUB, LANES)] * 2 + [vmem(2, 2, cap, SUB, LANES)] * STEPS + [
            pltpu.SMEM(new_global_slot.shape, jnp.int32),
            pltpu.SMEM(neighbors.shape, jnp.int32),
            pltpu.SemaphoreType.DMA((2,)),
            pltpu.SemaphoreType.DMA((4,)),
            pltpu.SemaphoreType.DMA((FIELDS, tiles, 2)),
            pltpu.SemaphoreType.DMA((FIELDS, tiles)),
            pltpu.SemaphoreType.DMA((FIELDS, tiles)),
            pltpu.SemaphoreType.DMA((4, EDGE)),
            pltpu.SemaphoreType.DMA((4, EDGE)),
            pltpu.SemaphoreType.DMA((STEPS, 2)),
            pltpu.SemaphoreType.DMA((STEPS, 2)),
        ],
        compiler_params=pltpu.CompilerParams(
            collective_id=0, has_side_effects=True, vmem_limit_bytes=44 * 1024 * 1024),
    )(*[pltpu.with_memory_space_constraint(table, pltpu.HBM) for table in (new_global_slot, neighbors)], tiled(old_phase), tiled(old_solute), tiled(old_mobility))
    last = vmem(cap * lag(STEPS - 1) * SUB, LANES)
    phase, solute = pl.pallas_call(
        functools.partial(finish, cap),
        out_shape=(jax.ShapeDtypeStruct((cap * rows, LANES), jnp.float32),) * 2,
        in_specs=[in_smem] + [in_vmem] * (3 + STEPS),
        out_specs=[anywhere] * 2,
        scratch_shapes=[vmem(2, cap, lag(t), SUB, LANES) for t in range(STEPS - 1)] + [last] * 2 + [
            pltpu.SemaphoreType.DMA((2, cap // SUB, 2 + lag(STEPS - 1)))],
        compiler_params=pltpu.CompilerParams(vmem_limit_bytes=32 * 1024 * 1024),
    )(neighbors, *[pltpu.with_memory_space_constraint(each, pltpu.VMEM) for each in state])
    return flat(phase), flat(solute)


def solution(mesh):
    placed = (P("blk", None), P("blk", None), P("blk", None), P("blk"), P("blk", None))
    return jax.shard_map(
        functools.partial(on_device, mesh.shape["blk"]),
        mesh=mesh,
        in_specs=placed,
        out_specs=(P("blk", None), P("blk", None)),
        check_vma=False,
    )
```

```python
import functools

import jax
import jax.numpy as jnp
from jax import lax
from jax.experimental import pallas as pl
from jax.experimental.pallas import tpu as pltpu
from jax.sharding import PartitionSpec as P

EDGE = 32
STEPS = 3
FIELDS = 3
SUB = 8
LANES = 128
AHEAD = 2
LAG = 3
SETTLE = 2
SLACK = 6
EARLY = 6
FIRST, LATE, CENTER = range(3)

time_step = 0.15
coupling = 1.5


def plane(k):
    half = k // 2 if isinstance(k, int) else lax.div(k, 2)
    if isinstance(k, int):
        return EDGE - 1 - half if k % 2 else half
    return jnp.where(lax.rem(k, 2) == 0, half, EDGE - 1 - half)


def lag(t):
    return 2 * (t + 1)


def stepper(cap, nbs, flds, mob, phi_out, conc_out, first):
    lane = lax.broadcasted_iota(jnp.int32, (SUB, LANES), 1)
    row = lax.broadcasted_iota(jnp.int32, (SUB, LANES), 0)
    z = lane % EDGE
    z_low, z_high = z == 0, z == EDGE - 1
    y_first, y_last = lane < EDGE, lane >= LANES - EDGE
    y_start, y_end = y_first & (row == 0), y_last & (row == SUB - 1)

    def local(column, b):
        index = nbs[b, column]
        return lax.rem(jnp.maximum(index, 0), cap), index >= 0

    def advance(t, b, x, beside):
        fld = flds[t]
        at_y0, has_y0 = local(2, b)
        at_y1, has_y1 = local(3, b)
        at_z0, _ = local(4, b)
        at_z1, _ = local(5, b)
        wall_y0 = y_start & jnp.logical_not(has_y0)
        wall_y1 = y_end & jnp.logical_not(has_y1)

        def laplacian(f, here):
            prev_x, next_x = beside(f)
            y0, y1 = fld[f, at_y0, x], fld[f, at_y1, x]
            z0, z1 = fld[f, at_z0, x], fld[f, at_z1, x]
            back = pltpu.roll(jnp.where(y_end, y0, here), EDGE, 1)
            prev_y = jnp.where(y_first, pltpu.roll(back, 1, 0), back)
            prev_y = jnp.where(wall_y0, here, prev_y)
            fore = pltpu.roll(jnp.where(y_start, y1, here), LANES - EDGE, 1)
            next_y = jnp.where(y_last, pltpu.roll(fore, SUB - 1, 0), fore)
            next_y = jnp.where(wall_y1, here, next_y)
            prev_z = jnp.where(z_low, pltpu.roll(z0, LANES - (EDGE - 1), 1), pltpu.roll(here, 1, 1))
            next_z = jnp.where(z_high, pltpu.roll(z1, EDGE - 1, 1), pltpu.roll(here, LANES - 1, 1))
            return (prev_x + next_x) + (prev_y + next_y) + (prev_z + next_z) - 6.0 * here

        phi, conc = fld[0, b, x], fld[1, b, x]
        wetting = 1.0 - phi * phi
        drive = laplacian(0, phi) + phi - phi * phi * phi - coupling * conc * wetting * wetting
        new_phi = phi + time_step * mob[b, x] * drive
        new_conc = conc + time_step * laplacian(1, conc) + 0.5 * (new_phi - phi)
        return new_phi, new_conc

    def keep(t, b, x, new_phi, new_conc):
        if t == STEPS - 1:
            at = b % SUB + (x - first) * (SUB * SUB) + (b // SUB) * (phi_out.shape[0] // (cap // SUB))
            phi_out[pl.ds(at, SUB, stride=SUB), :] = new_phi
            conc_out[pl.ds(at, SUB, stride=SUB), :] = new_conc
        else:
            flds[t + 1][0, b, x] = new_phi
            flds[t + 1][1, b, x] = new_conc

    def middle(t, k):
        x = plane(k)
        fld = flds[t]
        results = [advance(t, b, x, lambda f, b=b: (fld[f, b, x - 1], fld[f, b, x + 1])) for b in range(cap)]
        for b, result in enumerate(results):
            keep(t, b, x, *result)

    return local, advance, keep, middle


def kernel(n, cap, nold, ngs_ref, nbs_ref, op, oc, om, phi_out, conc_out, fld0, fld1, fld2, mob, early, late, center,
           side_s, side_r, pair_s, pair_r, far_s, far_r, near_s, near_r,
           cross_r, direct_r, ghost0, ghost1, ghost2, ngs, nbs, tsem, xsem, esem, lsem, msem, ssem, rsem, hs, hr):
    flds = (fld0, fld1, fld2)
    ghosts = (ghost0, ghost1, ghost2)
    sheet = SUB * SUB
    tiles = nold // SUB
    edge, inside = EARLY // 2, EDGE - EARLY
    early_loads, late_loads = [], []
    for f, src in enumerate((op, oc, om)):
        for q in range(tiles):
            for side in range(2):
                at = q * EDGE + side * (EDGE - edge)
                early_loads.append(pltpu.make_async_copy(
                    src.at[pl.ds(at * sheet, edge * sheet)],
                    early.at[pl.ds(((f * tiles + q) * EARLY + side * edge) * sheet, edge * sheet)], esem.at[f, q, side]))
            late_loads.append(pltpu.make_async_copy(
                src.at[pl.ds((q * EDGE + edge) * sheet, inside * sheet)],
                late.at[pl.ds((f * tiles + q) * inside * sheet, inside * sheet)], lsem.at[f, q]))
            early_loads.append(pltpu.make_async_copy(
                src.at[pl.ds((q * EDGE + plane(EDGE - 1)) * sheet, sheet)],
                center.at[pl.ds((f * tiles + q) * sheet, sheet)], msem.at[f, q]))
    tables = [
        pltpu.make_async_copy(src, dst, tsem.at[i])
        for i, (src, dst) in enumerate(((ngs_ref, ngs), (nbs_ref, nbs)))
    ]
    for copy in tables + early_loads + late_loads:
        copy.start()

    me = lax.axis_index("blk")
    core = me % 2
    odd = (me // 2) % 2
    sib = me + 1 - 2 * core
    near = me + 2 - 4 * odd
    far_final = me - 2 + 4 * odd
    far = me - 4 + 8 * odd
    far_source = me + 4 - 8 * odd
    side_final = me - 1 + 2 * core
    up, down = me + 1, me - 1
    has_up, has_down = up < n, down >= 0
    sends_far = (far_final >= 0) & (far_final < n)
    gets_far = (far_source >= 0) & (far_source < n)

    barrier = pltpu.get_barrier_semaphore()
    expected = jnp.int32(0)
    for other, there in ((up, has_up), (down, has_down), (near, None), (far, sends_far), (far_source, gets_far)):
        def greet(other=other):
            pl.semaphore_signal(barrier, inc=1, device_id=(other,), device_id_type=pl.DeviceIdType.MESH)
        if there is None:
            greet()
            expected = expected + 1
        else:
            pl.when(there)(greet)
            expected = expected + there.astype(jnp.int32)

    for copy in tables:
        copy.wait()
    start = ngs[0]
    count = jnp.int32(0)
    for s in range(nold):
        count = count + (ngs[s] >= 0).astype(jnp.int32)

    def held(part, k, final, put):
        x = plane(k)
        if part == CENTER:
            source, held_planes, at_plane = center, 1, 0
        elif part == FIRST:
            source, held_planes, at_plane = early, EARLY, jnp.where(x < edge, x, x - inside)
        else:
            source, held_planes, at_plane = late, inside, x - edge
        for j in range(cap):
            idx = final * cap + j - start
            mine = (idx >= 0) & (idx < count)
            idx = jnp.clip(idx, 0, nold - 1)
            row = lax.div(idx, SUB) * (held_planes * sheet) + lax.rem(idx, SUB) + at_plane * sheet
            for f in range(FIELDS):
                got = source[pl.ds(f * (tiles * held_planes * sheet) + row, SUB, stride=SUB), :]
                put(f, j, x, jnp.where(mine, got, 0.0))

    def link(stream, src, dst, k, target):
        return pltpu.make_async_remote_copy(
            src_ref=src.at[k], dst_ref=dst.at[k],
            send_sem=ssem.at[stream, k], recv_sem=rsem.at[stream, k],
            device_id=(target,), device_id_type=pl.DeviceIdType.MESH)

    def side_link(k):
        return link(0, side_s, side_r, k, sib)

    def pair_link(k):
        return link(1, pair_s, pair_r, k, sib)

    def far_link(k):
        return link(2, far_s, far_r, k, far)

    def near_link(k):
        return link(3, near_s, near_r, k, near)

    side_goes_far = (core + odd) % 2 == 1

    def fill(part, buffer, k, final):
        def put(f, j, x, value):
            buffer[k, f, j] = value
        held(part, k, final, put)

    def send_side(part, k):
        fill(part, side_s, k, side_final)
        side_link(k).start()

    def send_pair(part, k):
        fill(part, pair_s, k, sib)
        pair_link(k).start()

    def cross_link():
        return pltpu.make_async_remote_copy(
            src_ref=far_s.at[EDGE - 1], dst_ref=cross_r, send_sem=xsem.at[0], recv_sem=xsem.at[1],
            device_id=(near,), device_id_type=pl.DeviceIdType.MESH)

    def direct_link():
        return pltpu.make_async_remote_copy(
            src_ref=cross_r, dst_ref=direct_r, send_sem=xsem.at[2], recv_sem=xsem.at[3],
            device_id=(far_source,), device_id_type=pl.DeviceIdType.MESH)

    def add_side(k, total):
        side_link(k).wait_recv()
        total[k] += side_r[k]

    def send_far(part, k):
        fill(part, far_s, k, far_final)
        pl.when(side_goes_far)(lambda: add_side(k, far_s))
        pl.when(sends_far)(lambda: far_link(k).start())

    def send_near(part, k):
        fill(part, near_s, k, near)
        pl.when(jnp.logical_not(side_goes_far))(lambda: add_side(k, near_s))

        @pl.when(gets_far)
        def add_far():
            far_link(k).wait_recv()
            near_s[k] += far_r[k]

        near_link(k).start()

    def send_center():
        k = EDGE - 1

        @pl.when(side_goes_far)
        def near_first():
            near_link(k).start()
            add_side(k, far_s)
            pl.when(sends_far)(lambda: cross_link().start())

        @pl.when(jnp.logical_not(side_goes_far))
        def far_first():
            pl.when(sends_far)(lambda: cross_link().start())
            add_side(k, near_s)
            near_link(k).start()

    def hand_on():
        @pl.when(gets_far)
        def pass_center():
            cross_link().wait_recv()
            direct_link().start()

    def loop(lo, hi, *bodies):
        def body(i, carry):
            for each in bodies:
                each(i)
            return carry
        lax.fori_loop(lo, hi, body, 0)

    def pipeline(stages, hooks):
        cuts = set(hooks)
        for _, offset, size in stages:
            cuts |= {offset, offset + size}
        cuts = sorted(cuts)
        for lo, hi in zip(cuts, cuts[1:] + cuts[-1:]):
            for act in hooks.get(lo, ()):
                act()
            active = [(body, offset) for body, offset, size in stages if offset <= lo and hi <= offset + size]
            if lo < hi and active:
                loop(lo, hi, *[lambda i, body=body, offset=offset: body(i - offset) for body, offset in active])

    def settle(part, k):
        pair_link(k).wait_recv()
        near_link(k).wait_recv()
        if part == CENTER:
            @pl.when(sends_far)
            def add_direct():
                direct_link().wait_recv()
                near_r[k] += direct_r[...]

        def put(f, j, x, value):
            value = value + (pair_r[k, f, j] + near_r[k, f, j])
            if f < 2:
                fld0[f, j, x] = value
            else:
                mob[j, x] = value
        held(part, k, me, put)

    def sent(k):
        side_link(k).wait_send()
        pair_link(k).wait_send()
        near_link(k).wait_send()
        pl.when(sends_far)(lambda: far_link(k).wait_send())

    def ghost_link(t, side):
        return pltpu.make_async_remote_copy(
            src_ref=flds[t].at[:, :, 0 if side else EDGE - 1], dst_ref=ghosts[t].at[side],
            send_sem=hs.at[t, side], recv_sem=hr.at[t, side],
            device_id=(down if side else up,), device_id_type=pl.DeviceIdType.MESH)

    def start_ghosts(t):
        pl.when(has_up)(lambda: ghost_link(t, 0).start())
        pl.when(has_down)(lambda: ghost_link(t, 1).start())

    def await_ghosts(t):
        pl.when(has_down)(lambda: ghost_link(t, 0).wait_recv())
        pl.when(has_up)(lambda: ghost_link(t, 1).wait_recv())

    def await_sent(t):
        pl.when(has_up)(lambda: ghost_link(t, 0).wait_send())
        pl.when(has_down)(lambda: ghost_link(t, 1).wait_send())

    local, advance, keep, middle = stepper(cap, nbs, flds, mob, phi_out, conc_out, 0)

    def ends(t):
        fld, ghost, last = flds[t], ghosts[t], EDGE - 1
        await_ghosts(t)
        results = []
        for b in range(cap):
            at_x0, has_x0 = local(0, b)
            at_x1, has_x1 = local(1, b)
            results.append((b, 0, advance(t, b, 0, lambda f: (
                jnp.where(has_x0, ghost[0, f, at_x0], fld[f, b, 0]), fld[f, b, 1]))))
            results.append((b, last, advance(t, b, last, lambda f: (
                fld[f, b, last - 1], jnp.where(has_x1, ghost[1, f, at_x1], fld[f, b, last])))))
        for b, x, result in results:
            keep(t, b, x, *result)
        if t + 1 < STEPS:
            start_ghosts(t + 1)

    for copy in early_loads:
        copy.wait()
    for buffer, final in ((side_s, side_final), (near_s, near), (far_s, far_final)):
        fill(CENTER, buffer, EDGE - 1, final)
    pl.semaphore_wait(barrier, expected)
    near_at = AHEAD + LAG
    settle_at = near_at + SETTLE
    stages = []
    for body, offset in ((send_side, 0), (send_far, AHEAD), (send_near, near_at), (send_pair, near_at), (settle, settle_at)):
        stages.append((functools.partial(body, FIRST), offset, EARLY))
        size = EDGE if body is send_pair else EDGE - 1
        stages.append((lambda i, body=body: body(LATE, i + EARLY), offset + EARLY, size - EARLY))
    stages.append((lambda i: settle(CENTER, EDGE - 1), settle_at + EDGE - 1, 1))

    stages.append((sent, settle_at + 2, EDGE - 2))

    def await_late():
        for copy in late_loads:
            copy.wait()

    hooks = {
        0: (lambda: side_link(EDGE - 1).start(),),
        AHEAD + 1: (send_center,),
        EARLY: (await_late,),
        AHEAD + EDGE - 1: (hand_on,),
    }
    hooks[settle_at + 2] = hooks.get(settle_at + 2, ()) + (lambda: start_ghosts(0),)
    for t in range(STEPS):
        begin = settle_at + 2 + SLACK * t
        doubles = max(SLACK * t - lag(t), 0)
        if doubles:
            def two(i, t=t):
                middle(t, 2 * i + 2)
                middle(t, 2 * i + 3)
            stages.append((two, begin, doubles))
        done = 2 + 2 * doubles
        stages.append((lambda i, t=t, done=done: middle(t, i + done), settle_at + done + lag(t), EDGE - lag(t) - done))
        hooks[begin + SLACK] = hooks.get(begin + SLACK, ()) + (functools.partial(ends, t),)
    pipeline(stages, hooks)

    sent(EDGE - 2)
    for copy in (side_link(EDGE - 1), pair_link(EDGE - 1), near_link(EDGE - 1)):
        copy.wait_send()
    pl.when(sends_far)(lambda: cross_link().wait_send())
    pl.when(gets_far)(lambda: direct_link().wait_send())
    for t in range(STEPS):
        await_sent(t)


class Patched:
    def __init__(self, field, patch, first, size):
        self.field, self.patch, self.first, self.size = field, patch, first, size

    def __getitem__(self, at):
        f, b, x = at
        if self.first <= x < self.first + self.size:
            return self.patch[f, b, x - self.first]
        return self.field[f, b, x]

    def __setitem__(self, at, value):
        f, b, x = at
        self.patch[f, b, x - self.first] = value


def finish(cap, nbs, phi_ref, conc_ref, fld0, fld1, fld2, mob, phi_out, conc_out,
           new1, new2, phi_last, conc_last, sem):
    size = lag(STEPS - 1)
    first, sheet = (EDGE - size) // 2, SUB * SUB
    early, late = [], []
    for i, (ref, last, out) in enumerate(((phi_ref, phi_last, phi_out), (conc_ref, conc_last, conc_out))):
        for q in range(cap // SUB):
            for side, (lo, hi) in enumerate(((0, first), (first + size, EDGE))):
                at = pl.ds((q * EDGE + lo) * sheet, (hi - lo) * sheet)
                early.append(pltpu.make_async_copy(ref.at[at], out.at[at], sem.at[i, q, side]))
            for x in range(size):
                late.append((x, pltpu.make_async_copy(
                    last.at[pl.ds((q * size + x) * sheet, sheet)],
                    out.at[pl.ds((q * EDGE + first + x) * sheet, sheet)], sem.at[i, q, 2 + x])))
    for copy in early:
        copy.start()
    flds = [fld0]
    for t, (field, patch) in enumerate(((fld1, new1), (fld2, new2))):
        flds.append(Patched(field, patch, (EDGE - lag(t)) // 2, lag(t)))
    *_, middle = stepper(cap, nbs, flds, mob, phi_last, conc_last, first)
    for t in range(STEPS):
        for k in range(EDGE - lag(t), EDGE):
            middle(t, k)
            for x, copy in late:
                if t == STEPS - 1 and first + x == plane(k):
                    copy.start()
    for copy in early + [copy for _, copy in late]:
        copy.wait()


def on_device(n, old_phase, old_solute, old_mobility, new_global_slot, neighbors):
    cap = neighbors.shape[0]
    nold, cells = old_phase.shape
    rows = cells // LANES

    def tiled(field):
        split = field.reshape(nold // SUB, SUB, rows, LANES)
        return split.transpose(0, 2, 1, 3).reshape(nold * rows, LANES)

    def flat(field):
        split = field.reshape(cap // SUB, rows, SUB, LANES)
        return split.transpose(0, 2, 1, 3).reshape(cap, cells)

    def vmem(*shape):
        return pltpu.VMEM(shape, jnp.float32)

    in_vmem, anywhere = pl.BlockSpec(memory_space=pltpu.VMEM), pl.BlockSpec(memory_space=pl.ANY)
    in_smem = pl.BlockSpec(memory_space=pltpu.SMEM)
    field = vmem(2, cap, EDGE, SUB, LANES)
    buffer = vmem(EDGE, FIELDS, cap, SUB, LANES)
    tiles, sheet = nold // SUB, SUB * SUB
    state = pl.pallas_call(
        functools.partial(kernel, n, cap, nold),
        out_shape=(vmem(cap * rows, LANES),) * 2 + (field,) * STEPS + (vmem(cap, EDGE, SUB, LANES),),
        in_specs=[anywhere] * 5,
        out_specs=[in_vmem] * (3 + STEPS),
        scratch_shapes=[vmem(FIELDS * tiles * EARLY * sheet, LANES), vmem(FIELDS * tiles * (EDGE - EARLY) * sheet, LANES)]
        + [vmem(FIELDS * tiles * sheet, LANES)] + [buffer] * 8 + [vmem(FIELDS, cap, SUB, LANES)] * 2 + [vmem(2, 2, cap, SUB, LANES)] * STEPS + [
            pltpu.SMEM(new_global_slot.shape, jnp.int32),
            pltpu.SMEM(neighbors.shape, jnp.int32),
            pltpu.SemaphoreType.DMA((2,)),
            pltpu.SemaphoreType.DMA((4,)),
            pltpu.SemaphoreType.DMA((FIELDS, tiles, 2)),
            pltpu.SemaphoreType.DMA((FIELDS, tiles)),
            pltpu.SemaphoreType.DMA((FIELDS, tiles)),
            pltpu.SemaphoreType.DMA((4, EDGE)),
            pltpu.SemaphoreType.DMA((4, EDGE)),
            pltpu.SemaphoreType.DMA((STEPS, 2)),
            pltpu.SemaphoreType.DMA((STEPS, 2)),
        ],
        compiler_params=pltpu.CompilerParams(
            collective_id=0, has_side_effects=True, vmem_limit_bytes=44 * 1024 * 1024),
    )(*[pltpu.with_memory_space_constraint(table, pltpu.HBM) for table in (new_global_slot, neighbors)], tiled(old_phase), tiled(old_solute), tiled(old_mobility))
    last = vmem(cap * lag(STEPS - 1) * SUB, LANES)
    phase, solute = pl.pallas_call(
        functools.partial(finish, cap),
        out_shape=(jax.ShapeDtypeStruct((cap * rows, LANES), jnp.float32),) * 2,
        in_specs=[in_smem] + [in_vmem] * (3 + STEPS),
        out_specs=[anywhere] * 2,
        scratch_shapes=[vmem(2, cap, lag(t), SUB, LANES) for t in range(STEPS - 1)] + [last] * 2 + [
            pltpu.SemaphoreType.DMA((2, cap // SUB, 2 + lag(STEPS - 1)))],
        compiler_params=pltpu.CompilerParams(vmem_limit_bytes=32 * 1024 * 1024),
    )(neighbors, *[pltpu.with_memory_space_constraint(each, pltpu.VMEM) for each in state])
    return flat(phase), flat(solute)


def solution(mesh):
    placed = (P("blk", None), P("blk", None), P("blk", None), P("blk"), P("blk", None))
    return jax.shard_map(
        functools.partial(on_device, mesh.shape["blk"]),
        mesh=mesh,
        in_specs=placed,
        out_specs=(P("blk", None), P("blk", None)),
        check_vma=False,
    )
```
